256 devices in a mesh: cuts: 8 (over x, y_lo), layer: 32 (over z, y_hi, core).
Axes of the slice: x: 4, y: 4 (y_hi: 2, y_lo: 2; y = y_hi * 2 + y_lo), z: 8, core: 2. Of those that a mesh axis runs over, the one named last changes fastest.
Arguments:
- vectors: float32 [8, 64, 64, 1024], P('cuts', None, 'layer'), may hold values from -40 to 40
- diag_blocks: bfloat16 [64, 1024, 1024], P('layer'), may hold values from -1 to 1, as said below
- couplings: bfloat16 [64, 1024, 1024], P('layer'), may hold values from -0.09375 to 0.09375
- bounds: int32 [8, 2], P('cuts'), may hold values from -128 to 160, as said below
Outputs:
- filtered: float32 [8, 64, 64, 1024], P('cuts', None, 'layer')
The draws below stay inside these ranges and needn't reach their ends.
Inputs may be any that keep to these rules, and one draw needn't show every extreme that they name: `bounds`: column 0 holds each slice's lower end, which is -128 at slice 0 and to at most -81; column 1 holds its upper end, from 128 to 160. `diag_blocks`: each block is symmetric.
All inputs are finite; a program needn't handle non-finite values.
Results may differ from the reference program's by a relative error of at most 0.012.
Values may be sent and summed in bfloat16 or wider, within the bound.
A program may use at most 64 MiB of HBM per device.

```python
import math
import jax
import jax.numpy as jnp
from jax import lax

B = 1024
K = 64
EDGE = 16
DEG = 4
STEPS = 2
SLICES = 8
NL = 64
ORDER = 65536


def draw_bounds(key, part):
    first_key, second_key = jax.random.split(jax.random.fold_in(key, 11))
    slice_index = jnp.arange(SLICES).astype(jnp.int32)
    rising = 40 * slice_index // max(SLICES - 1, 1)
    jitter = jax.random.randint(first_key, (SLICES,), 0, 8) * (slice_index > 0).astype(jnp.int32)
    bottom = -128 + rising + jitter
    summit = jax.random.randint(second_key, (SLICES,), 128, 161)
    return jnp.stack([bottom, summit], 1).astype(jnp.int32)


def draw_diag_blocks(key, part):
    inner_key = jax.random.fold_in(key, 23)
    raw = jax.random.normal(inner_key, (NL, B, B), jnp.float32)
    symmetric = (raw + jnp.swapaxes(raw, 1, 2)) / (2.0 * math.sqrt(B))
    return jnp.clip(symmetric, -1.0, 1.0).astype(jnp.bfloat16)


def draw_vectors(key, part):
    keys = jax.random.split(jax.random.fold_in(key, 37), 3)
    layer_pos = jnp.arange(NL).astype(jnp.float32) / max(NL - 1, 1)
    own = jax.random.normal(keys[0], (SLICES, K, NL, B), jnp.float32)
    shared = jax.random.normal(keys[1], (SLICES, EDGE, NL, B), jnp.float32)
    spread = jnp.exp(jax.random.uniform(keys[2], (NL,), jnp.float32, 0.0, math.log(3.2)))
    rising = jnp.sqrt(1.0 + 2.0 * layer_pos)
    block = 0.6 * own
    block = block.at[:, :EDGE].add(0.8 * jnp.roll(shared, 1, 0))
    block = block.at[:, K - EDGE:].add(0.8 * shared)
    scale = (rising * spread).reshape(1, 1, NL, 1)
    return jnp.clip(block * scale, -40.0, 40.0).astype(jnp.float32)


def block_levels(key, shape, shards, low, high):
    def one(axis_at, shards_of):
        heights = jax.random.uniform(jax.random.fold_in(jax.random.fold_in(key, 6), axis_at), (shards_of,), jnp.float32, low / len(shards), high / len(shards))
        return jnp.repeat(jnp.exp(heights), shape[axis_at] // shards_of).reshape((-1,) + (1,) * (len(shape) - axis_at - 1))

    level = one(*shards[0])
    for cut in shards[1:]:
        level = level * one(*cut)
    return level


def centred(rng, dims, scale, reach, cuts=(), held_as=jnp.bfloat16):
    values = scale * jax.random.normal(rng, dims, jnp.float32)
    if cuts:
        values = values * block_levels(rng, dims, cuts, -0.22, 0.18)
    return jnp.clip(values, -reach, reach).astype(held_as)


def setup_inputs(seed: int = 0) -> dict:
    streams_of = jax.random.split(jax.random.key(seed), 5)
    return {
        "vectors": draw_vectors(jax.random.fold_in(streams_of[4], 71), 0),
        "diag_blocks": draw_diag_blocks(jax.random.fold_in(streams_of[4], 71), 0),
        "couplings": centred(streams_of[2], (NL, B, B), (4 * B) ** -0.5, 0.09375, ((0, 32),)),
        "bounds": draw_bounds(jax.random.fold_in(streams_of[4], 71), 0),
    }


def apply_hamiltonian(vectors_now, blocks_diag, blocks_link):
    rounded = lax.optimization_barrier(vectors_now.astype(jnp.bfloat16)).astype(jnp.float32)
    result = jnp.einsum('skld,lde->skle', rounded, blocks_diag, precision=lax.Precision.HIGHEST)
    upward = jnp.einsum('skle,lde->skld', rounded[:, :, 1:], blocks_link[:-1], precision=lax.Precision.HIGHEST)
    downward = jnp.einsum('skld,lde->skle', rounded[:, :, :-1], blocks_link[:-1], precision=lax.Precision.HIGHEST)
    zero_layer = jnp.zeros_like(rounded[:, :, :1])
    result = result + jnp.concatenate([upward, zero_layer], 2)
    return result + jnp.concatenate([zero_layer, downward], 2)

def filter_step(start, centre, half_width, blocks_diag, blocks_link):
    previous = start
    current = (apply_hamiltonian(start, blocks_diag, blocks_link) - centre * start) / half_width
    for degree_index in range(DEG - 1):
        following = 2.0 * (apply_hamiltonian(current, blocks_diag, blocks_link) - centre * current) / half_width - previous
        previous = current
        current = following
    return current

def orthonormal(filtered_block):
    flat = filtered_block.reshape(SLICES, K, ORDER)
    gram = jnp.einsum('skn,sjn->skj', flat, flat, precision=lax.Precision.HIGHEST) / ORDER
    factor = jnp.linalg.cholesky(gram)
    solved = lax.linalg.triangular_solve(factor, flat, left_side=True, lower=True)
    return solved

def reference(vectors, diag_blocks, couplings, bounds):
    blocks_diag = diag_blocks.astype(jnp.float32)
    blocks_link = couplings.astype(jnp.float32)
    bottom = bounds[:, 0].astype(jnp.float32) / 64.0
    summit = bounds[:, 1].astype(jnp.float32) / 64.0
    centre = ((bottom + summit) / 2.0).reshape(SLICES, 1, 1, 1)
    half_width = ((summit - bottom) / 2.0).reshape(SLICES, 1, 1, 1)
    current_block = vectors
    for repeat in range(STEPS):
        filtered_block = filter_step(current_block, centre, half_width, blocks_diag, blocks_link)
        final = orthonormal(filtered_block)
        current_block = final.reshape(SLICES, K, NL, B)
    low_edge = final[:, :EDGE]
    high_edge = final[:, K - EDGE:]
    zero_slice = jnp.zeros_like(low_edge[:1])
    below_high = jnp.concatenate([zero_slice, high_edge[:-1]], 0)
    above_low = jnp.concatenate([low_edge[1:], zero_slice], 0)
    correlation_low = jnp.einsum('swn,svn->swv', below_high, low_edge, precision=lax.Precision.HIGHEST) / ORDER
    correlation_high = jnp.einsum('swn,svn->swv', above_low, high_edge, precision=lax.Precision.HIGHEST) / ORDER
    low_new = low_edge - jnp.einsum('swv,swn->svn', correlation_low, below_high, precision=lax.Precision.HIGHEST)
    high_new = high_edge - jnp.einsum('swv,swn->svn', correlation_high, above_low, precision=lax.Precision.HIGHEST)
    result = jnp.concatenate([low_new, final[:, EDGE:K - EDGE], high_new], 1)
    return result.reshape(SLICES, K, NL, B)
```

```python
import functools

import jax
import jax.numpy as jnp
from jax import lax
from jax.experimental import pallas as pl
from jax.experimental.pallas import tpu as pltpu
from jax.sharding import PartitionSpec as P

EDGE = 16
DEG = 4
STEPS = 2
GROUP = 4
F32 = jnp.float32
BF16 = jnp.bfloat16
NN = (((1,), (0,)), ((), ()))
NT = (((1,), (1,)), ((), ()))
TN = (((0,), (0,)), ((), ()))
MESH = pl.DeviceIdType.MESH


def mm(a, b, dims=NN):
    return lax.dot_general(a, b, dims, preferred_element_type=F32)


def split(value):
    high = value.astype(BF16)
    return high, (value - high.astype(F32)).astype(BF16)


def cholesky_inverse(gram):
    n = gram.shape[0]
    rows = lax.broadcasted_iota(jnp.int32, (n, n), 0)
    lanes = lax.broadcasted_iota(jnp.int32, (n, n), 1)
    eye = (rows == lanes).astype(F32)
    whole = jnp.concatenate([gram, eye], axis=1)
    blocks = [whole[8 * b : 8 * b + 8] for b in range(n // 8)]
    inner = lax.broadcasted_iota(jnp.int32, (8, 2 * n), 0)
    for j in range(n):
        home = j // 8
        row = jnp.broadcast_to(blocks[home][j % 8 : j % 8 + 1], (8, 2 * n))
        pivot = jnp.broadcast_to(row[:, j : j + 1], (8, 2 * n))
        scaled = row / pivot
        for b in range(home, n // 8):
            column = jnp.broadcast_to(blocks[b][:, j : j + 1], (8, 2 * n))
            if b == home:
                column = jnp.where(inner > j % 8, column, 0.0)
            blocks[b] = blocks[b] - column * scaled
    whole = jnp.concatenate(blocks, axis=0)
    diagonal = jnp.sum(whole[:, :n] * eye, axis=1, keepdims=True)
    return whole[:, n:] * lax.rsqrt(diagonal)


def kernel(
    sizes, bounds, x_in, d_hbm, c_hbm, out,
    dv, cv, zf, zb, pb, rz, rp, acc, own, first, second, edge_out, edge_in,
    load_sem, zs, zr, ps, pr, a1s, a1r, a2s, a2r, es, er,
):
    n_cuts, n_layer = sizes
    n_z = n_layer // GROUP
    me = lax.axis_index("layer")
    cut = lax.axis_index("cuts")
    plane, member = me // GROUP, me % GROUP
    k, width = x_in.shape[1:]
    half = width // 2
    length_all = n_layer * 2 * width
    has_prev, has_next = me > 0, me < n_layer - 1
    has_below, has_above = cut > 0, cut < n_cuts - 1
    group_peer = [plane * GROUP + (member + q) % GROUP for q in range(1, GROUP)]
    plane_peer = [((plane + q) % n_z) * GROUP + member for q in range(1, n_z)]

    loads = []
    for i, (src, dst) in enumerate(((c_hbm, cv), (d_hbm, dv))):
        for l in (1, 0):
            loads.append(pltpu.make_async_copy(src.at[l], dst.at[l], load_sem.at[2 * i + l]))
    for copy in loads:
        copy.start()

    barrier = pltpu.get_barrier_semaphore()

    def greet(condition, device):
        @pl.when(condition)
        def _():
            pl.semaphore_signal(barrier, inc=1, device_id=device, device_id_type=MESH)

    for peer in group_peer + plane_peer:
        pl.semaphore_signal(barrier, inc=1, device_id={"layer": peer}, device_id_type=MESH)
    greet(has_prev, {"layer": me - 1})
    greet(has_next, {"layer": me + 1})
    greet(has_below, {"cuts": cut - 1})
    greet(has_above, {"cuts": cut + 1})

    low = bounds[0, 0].astype(F32) / 64.0
    high = bounds[0, 1].astype(F32) / 64.0
    centre = jnp.full((8, 128), (low + high) / 2.0, F32)[:1, :1]
    inverse = 1.0 / jnp.full((8, 128), (high - low) / 2.0, F32)[:1, :1]

    for l in range(2):
        zf[0, l] = x_in[l]
        zf[1, l] = jnp.zeros((k, width), F32)
        zb[0, l] = x_in[l].astype(BF16)

    @pl.when(jnp.logical_not(has_next))
    def _():
        rz[...] = jnp.zeros_like(rz)

    @pl.when(jnp.logical_not(has_prev))
    def _():
        rp[...] = jnp.zeros_like(rp)

    @pl.when(jnp.logical_not(has_below))
    def _():
        edge_in[0] = jnp.zeros_like(edge_in[0])

    @pl.when(jnp.logical_not(has_above))
    def _():
        edge_in[1] = jnp.zeros_like(edge_in[1])

    signals = (GROUP - 1) + (n_z - 1)
    for condition in (has_prev, has_next, has_below, has_above):
        signals = signals + jnp.where(condition, 1, 0)
    pl.semaphore_wait(barrier, signals)
    for copy in loads:
        copy.wait()

    def z_copy(t):
        return pltpu.make_async_remote_copy(
            zb.at[t, 0], rz.at[t], zs.at[t], zr.at[t],
            device_id={"layer": me - 1}, device_id_type=MESH,
        )

    def p_copy(t):
        return pltpu.make_async_remote_copy(
            pb.at[t], rp.at[t], ps.at[t], pr.at[t],
            device_id={"layer": me + 1}, device_id_type=MESH,
        )

    columns = [pl.ds(h * half, half) for h in range(2)]

    def apply_step(t, factor, back):
        cur, nxt = t % 2, (t + 1) % 2

        @pl.when(has_prev)
        def _():
            z_copy(t).start()

        for s in columns:
            pb[t, :, s] = mm(zb[t, 1], cv[1, :, s]).astype(BF16)

        @pl.when(has_next)
        def _():
            p_copy(t).start()

        for s in columns:
            acc[0, :, s] = mm(zb[t, 0], dv[0, :, s]) + mm(zb[t, 1], cv[0, s, :], NT)
            acc[1, :, s] = mm(zb[t, 1], dv[1, :, s]) + mm(zb[t, 0], cv[0, :, s])

        def update(l, s, total):
            now = zf[cur, l, :, s]
            value = (factor * inverse) * (total - centre * now) - back * zf[nxt, l, :, s]
            zf[nxt, l, :, s] = value
            zb[t + 1, l, :, s] = value.astype(BF16)

        @pl.when(has_next)
        def _():
            z_copy(t).wait_recv()

        for s in columns:
            update(1, s, acc[1, :, s] + mm(rz[t], cv[1, s, :], NT))

        @pl.when(has_prev)
        def _():
            p_copy(t).wait_recv()

        for s in columns:
            update(0, s, acc[0, :, s] + rp[t, :, s].astype(F32))

    def all_reduce(i, value):
        own[i, 0] = value
        sends = []
        for q, peer in enumerate(group_peer):
            sends.append(pltpu.make_async_remote_copy(
                own.at[i, 0], first.at[i, q], a1s.at[i, q], a1r.at[i, q],
                device_id={"layer": peer}, device_id_type=MESH,
            ))
        for copy in sends:
            copy.start()
        for copy in sends:
            copy.wait_recv()
        total = value
        for q in range(GROUP - 1):
            total = total + first[i, q]
        own[i, 1] = total
        more = []
        for q, peer in enumerate(plane_peer):
            more.append(pltpu.make_async_remote_copy(
                own.at[i, 1], second.at[i, q], a2s.at[i, q], a2r.at[i, q],
                device_id={"layer": peer}, device_id_type=MESH,
            ))
        for copy in more:
            copy.start()
        for copy in more:
            copy.wait_recv()
        for q in range(n_z - 1):
            total = total + second[i, q]
        for copy in sends + more:
            copy.wait_send()
        return total

    def orthonormal(i, src, store):
        gram = jnp.zeros((2 * k, 2 * k), F32)
        for l in range(2):
            pair = jnp.concatenate(split(zf[src, l]), axis=0)
            gram = gram + mm(pair, pair, NT)
        gram = gram[:k, :k] + gram[:k, k:] + gram[k:, :k]
        packed = jnp.concatenate([gram[: k // 2], gram[k // 2 :]], axis=1)
        packed = all_reduce(i, packed)
        gram = jnp.concatenate([packed[:, :k], packed[:, k:]], axis=0) * (1.0 / length_all)
        factor_high, factor_low = split(cholesky_inverse(gram))
        factors = jnp.concatenate([factor_high, factor_high, factor_low], axis=1)
        for l in range(2):
            y_high, y_low = split(zf[src, l])
            store(l, mm(factors, jnp.concatenate([y_high, y_low, y_high], axis=0)))

    def factor_of(t):
        return jnp.where(t == 0, 1.0, 2.0), jnp.where(t == 0, 0.0, 1.0)

    def first_filter(t, carry):
        apply_step(t, *factor_of(t))
        return carry

    def second_filter(t, carry):
        apply_step(t + DEG, *factor_of(t))
        return carry

    lax.fori_loop(0, DEG, first_filter, 0)

    def store_first(l, value):
        zf[0, l] = value
        zf[1, l] = jnp.zeros((k, width), F32)
        zb[DEG, l] = value.astype(BF16)

    orthonormal(0, 0, store_first)
    lax.fori_loop(0, DEG, second_filter, 0)

    def store_last(l, value):
        out[l] = value
        edge_out[0, l] = value[k - EDGE :].astype(BF16)
        edge_out[1, l] = value[:EDGE].astype(BF16)

    orthonormal(1, 0, store_last)

    to_above = pltpu.make_async_remote_copy(
        edge_out.at[0], edge_in.at[0], es.at[0], er.at[0],
        device_id={"cuts": cut + 1}, device_id_type=MESH,
    )
    to_below = pltpu.make_async_remote_copy(
        edge_out.at[1], edge_in.at[1], es.at[1], er.at[1],
        device_id={"cuts": cut - 1}, device_id_type=MESH,
    )
    pl.when(has_above)(to_above.start)
    pl.when(has_below)(to_below.start)
    pl.when(has_below)(to_above.wait_recv)
    pl.when(has_above)(to_below.wait_recv)

    edges = (slice(0, EDGE), slice(k - EDGE, k))
    parts = []
    for side in range(2):
        part = jnp.zeros((EDGE, EDGE), F32)
        for l in range(2):
            e_high, e_low = split(out[l, edges[side], :])
            other = edge_in[side, l]
            part = part + mm(other, e_high, NT) + mm(other, e_low, NT)
        parts.append(part)
    filler = jnp.zeros((EDGE, 128 - 2 * EDGE), F32)
    sums = jnp.concatenate(parts + [filler], axis=1)
    own_rows = own.shape[2]
    sums = jnp.concatenate([sums, jnp.zeros((own_rows - EDGE, 128), F32)], axis=0)
    sums = all_reduce(2, sums) * (1.0 / length_all)
    for side in range(2):
        c_high, c_low = split(sums[:EDGE, side * EDGE : (side + 1) * EDGE])
        for l in range(2):
            other = edge_in[side, l]
            out[l, edges[side], :] = (
                out[l, edges[side], :] - mm(c_high, other, TN) - mm(c_low, other, TN)
            )

    pl.when(has_above)(to_above.wait_send)
    pl.when(has_below)(to_below.wait_send)

    def drain(t, carry):
        pl.when(has_prev)(z_copy(t).wait_send)
        pl.when(has_next)(p_copy(t).wait_send)
        return carry

    lax.fori_loop(0, STEPS * DEG, drain, 0)


def per_device(sizes, vectors, diag_blocks, couplings, bounds):
    x = jnp.transpose(vectors[0], (1, 0, 2))
    _, k, width = x.shape
    n_z = sizes[1] // GROUP
    runs = STEPS * DEG
    vmem = pl.BlockSpec(memory_space=pltpu.VMEM)
    anywhere = pl.BlockSpec(memory_space=pl.ANY)
    dma = pltpu.SemaphoreType.DMA
    result = pl.pallas_call(
        functools.partial(kernel, sizes),
        out_shape=jax.ShapeDtypeStruct(x.shape, F32),
        in_specs=[pl.BlockSpec(memory_space=pltpu.SMEM), vmem, anywhere, anywhere],
        out_specs=vmem,
        scratch_shapes=[
            pltpu.VMEM((2, width, width), BF16),
            pltpu.VMEM((2, width, width), BF16),
            pltpu.VMEM((2, 2, k, width), F32),
            pltpu.VMEM((runs + 1, 2, k, width), BF16),
            pltpu.VMEM((runs, k, width), BF16),
            pltpu.VMEM((runs, k, width), BF16),
            pltpu.VMEM((runs, k, width), BF16),
            pltpu.VMEM((2, k, width), F32),
            pltpu.VMEM((3, 2, k // 2, 128), F32),
            pltpu.VMEM((3, GROUP - 1, k // 2, 128), F32),
            pltpu.VMEM((3, n_z - 1, k // 2, 128), F32),
            pltpu.VMEM((2, 2, EDGE, width), BF16),
            pltpu.VMEM((2, 2, EDGE, width), BF16),
            dma((4,)),
            dma((runs,)),
            dma((runs,)),
            dma((runs,)),
            dma((runs,)),
            dma((3, GROUP - 1)),
            dma((3, GROUP - 1)),
            dma((3, n_z - 1)),
            dma((3, n_z - 1)),
            dma((2,)),
            dma((2,)),
        ],
        compiler_params=pltpu.CompilerParams(
            collective_id=0, has_side_effects=True, vmem_limit_bytes=48 << 20
        ),
    )(bounds, x, diag_blocks, couplings)
    return jnp.transpose(result, (1, 0, 2))[None]


def solution(mesh):
    sizes = (mesh.shape["cuts"], mesh.shape["layer"])
    in_specs = (
        P("cuts", None, "layer", None),
        P("layer", None, None),
        P("layer", None, None),
        P("cuts", None),
    )
    return jax.shard_map(
        functools.partial(per_device, sizes),
        mesh=mesh,
        in_specs=in_specs,
        out_specs=P("cuts", None, "layer", None),
        check_vma=False,
    )
```

```python
import functools

import jax
import jax.numpy as jnp
from jax import lax
from jax.experimental import pallas as pl
from jax.experimental.pallas import tpu as pltpu
from jax.sharding import PartitionSpec as P

EDGE = 16
DEG = 4
STEPS = 2
GROUP = 4
F32 = jnp.float32
BF16 = jnp.bfloat16
NN = (((1,), (0,)), ((), ()))
NT = (((1,), (1,)), ((), ()))
TN = (((0,), (0,)), ((), ()))
MESH = pl.DeviceIdType.MESH


def mm(a, b, dims=NN):
    return lax.dot_general(a, b, dims, preferred_element_type=F32)


def split(value):
    high = value.astype(BF16)
    return high, (value - high.astype(F32)).astype(BF16)


def cholesky_inverse(gram, group=4):
    n = gram.shape[0]
    rows_at = lax.broadcasted_iota(jnp.int32, (n, n), 0)
    lanes_at = lax.broadcasted_iota(jnp.int32, (n, n), 1)
    eye = (rows_at == lanes_at).astype(F32)
    whole = jnp.concatenate([gram, eye], axis=1)
    shape = (8, 2 * n)
    blocks = [whole[8 * b : 8 * b + 8] for b in range(n // 8)]
    inner = lax.broadcasted_iota(jnp.int32, shape, 0)
    for j in range(0, n, group):
        home, at = j // 8, j % 8
        active = range(home, n // 8)
        rows = [jnp.broadcast_to(blocks[home][at + i : at + i + 1], shape) for i in range(group)]
        cross = {
            (i, m): jnp.broadcast_to(rows[i][:, j + m : j + m + 1], shape)
            for i in range(group)
            for m in range(i, group)
        }
        columns = {
            (b, i): jnp.broadcast_to(blocks[b][:, j + i : j + i + 1], shape)
            for b in active
            for i in range(group)
        }
        for i in range(group):
            inverse = 1.0 / cross[i, i]
            scaled = rows[i] * inverse
            later = range(i + 1, group)
            ratio = {m: cross[i, m] * inverse for m in later}
            for m in later:
                rows[m] = rows[m] - cross[i, m] * scaled
                for q in range(m, group):
                    cross[m, q] = cross[m, q] - cross[i, m] * ratio[q]
            for b in active:
                column = columns[b, i]
                for m in later:
                    columns[b, m] = columns[b, m] - column * ratio[m]
                if b == home:
                    column = jnp.where(inner > at + i, column, 0.0)
                blocks[b] = blocks[b] - column * scaled
    whole = jnp.concatenate(blocks, axis=0)
    diagonal = jnp.sum(whole[:, :n] * eye, axis=1, keepdims=True)
    return whole[:, n:] * lax.rsqrt(diagonal)


def stacked_factor(factor):
    high, low = split(factor)
    return jnp.concatenate([high, high, low], axis=1)


def stacked_rows(rows):
    high, low = split(rows)
    return jnp.concatenate([high, low, high], axis=0)


def exact(a, b, dims):
    return lax.dot_general(
        a, b, dims, precision=lax.Precision.HIGHEST, preferred_element_type=F32
    )


def kernel(
    sizes, bounds_hbm, x_in, d_hbm, c_hbm, out,
    bounds, dv, cv, ct, zf, zb, pb, rz, rp, acc, own, first, second, factors,
    ylow_out, ylow_in, high_out, high_in, corr_out, corr_in,
    load_sem, zs, zr, ps, pr, a1s, a1r, a2s, a2r, es, er,
):
    n_cuts, n_layer = sizes
    n_z = n_layer // GROUP
    me = lax.axis_index("layer")
    cut = lax.axis_index("cuts")
    plane, member = me // GROUP, me % GROUP
    k, width = x_in.shape[1:]
    half = width // 2
    scale = 1.0 / (n_layer * 2 * width)
    has_prev, has_next = me > 0, me < n_layer - 1
    has_below, has_above = cut > 0, cut < n_cuts - 1
    group_peer = [plane * GROUP + (member + q) % GROUP for q in range(1, GROUP)]
    plane_peer = [((plane + q) % n_z) * GROUP + member for q in range(1, n_z)]

    bounds_load = pltpu.make_async_copy(bounds_hbm, bounds, load_sem.at[4])
    bounds_load.start()
    loads = []
    for i, (src, dst) in enumerate(((c_hbm, cv), (d_hbm, dv))):
        for l in (1, 0):
            loads.append(pltpu.make_async_copy(src.at[l], dst.at[l], load_sem.at[2 * i + l]))
    for copy in loads:
        copy.start()

    barrier = pltpu.get_barrier_semaphore()

    def greet(condition, device):
        @pl.when(condition)
        def _():
            pl.semaphore_signal(barrier, inc=1, device_id=device, device_id_type=MESH)

    for peer in plane_peer + group_peer:
        pl.semaphore_signal(barrier, inc=1, device_id={"layer": peer}, device_id_type=MESH)
    greet(has_prev, {"layer": me - 1})
    greet(has_next, {"layer": me + 1})
    greet(has_below, {"cuts": cut - 1})
    greet(has_above, {"cuts": cut + 1})

    for l in range(2):
        zf[0, l] = x_in[l]
        zf[1, l] = jnp.zeros((k, width), F32)
        zb[0, l] = x_in[l].astype(BF16)

    @pl.when(jnp.logical_not(has_next))
    def _():
        rz[...] = jnp.zeros_like(rz)

    @pl.when(jnp.logical_not(has_prev))
    def _():
        rp[...] = jnp.zeros_like(rp)

    @pl.when(jnp.logical_not(has_below))
    def _():
        high_in[...] = jnp.zeros_like(high_in)
        corr_in[...] = jnp.zeros_like(corr_in)

    @pl.when(jnp.logical_not(has_above))
    def _():
        ylow_in[...] = jnp.zeros_like(ylow_in)

    bounds_load.wait()
    low = bounds[0, 0].astype(F32) / 64.0
    high = bounds[0, 1].astype(F32) / 64.0
    centre = jnp.full((8, 128), (low + high) / 2.0, F32)[:1, :1]
    inverse = 1.0 / jnp.full((8, 128), (high - low) / 2.0, F32)[:1, :1]
    for copy in loads:
        copy.wait()
    for l in (1, 0):
        ct[l] = jnp.transpose(cv[l])

    signals = (GROUP - 1) + (n_z - 1)
    for condition in (has_prev, has_next, has_below, has_above):
        signals = signals + jnp.where(condition, 1, 0)
    pl.semaphore_wait(barrier, signals)

    columns = [pl.ds(h * half, half) for h in range(2)]

    def remote(src, dst, send, recv, device):
        return pltpu.make_async_remote_copy(
            src, dst, send, recv, device_id=device, device_id_type=MESH
        )

    def z_copy(t, h):
        return remote(
            zb.at[t, 0, :, columns[h]], rz.at[t, :, columns[h]], zs.at[t, h], zr.at[t, h],
            {"layer": me - 1},
        )

    def p_copy(t, h):
        return remote(
            pb.at[t, h], rp.at[t, h], ps.at[t, h], pr.at[t, h], {"layer": me + 1}
        )

    def group_copy(i, q):
        return remote(
            own.at[i, 0], first.at[i, q], a1s.at[i, q], a1r.at[i, q], {"layer": group_peer[q]}
        )

    def plane_copy(i, q):
        return remote(
            own.at[i, 1], second.at[i, q], a2s.at[i, q], a2r.at[i, q], {"layer": plane_peer[q]}
        )

    def reduce_start(i, value):
        own[i, 0] = value
        for q in range(GROUP - 1):
            group_copy(i, q).start()

    def reduce_middle(i):
        for q in range(GROUP - 1):
            group_copy(i, q).wait_recv()
        total = own[i, 0]
        for q in range(GROUP - 1):
            total = total + first[i, q]
        own[i, 1] = total
        for q in range(n_z - 1):
            plane_copy(i, q).start()

    def reduce_end(i):
        for q in range(n_z - 1):
            plane_copy(i, q).wait_recv()
        total = own[i, 1]
        for q in range(n_z - 1):
            total = total + second[i, q]
        return total

    def gram_start(i, src):
        gram = jnp.zeros((2 * k, 2 * k), F32)
        for l in range(2):
            pair = jnp.concatenate(split(zf[src, l]), axis=0)
            gram = gram + mm(pair, pair, NT)
        gram = gram[:k, :k] + gram[:k, k:] + gram[k:, :k]
        reduce_start(i, jnp.concatenate([gram[: k // 2], gram[k // 2 :]], axis=1))

    def gram_end(i):
        packed = reduce_end(i)
        return jnp.concatenate([packed[:, :k], packed[:, k:]], axis=0) * scale

    def apply_step(t, carry):
        cur, nxt = t % 2, (t + 1) % 2
        opening = t % DEG == 0
        factor, back = jnp.where(opening, 1.0, 2.0), jnp.where(opening, 0.0, 1.0)

        @pl.when(has_prev)
        def _():
            z_copy(t, 0).start()
            z_copy(t, 1).start()

        for h, s in enumerate(columns):
            pb[t, h] = mm(zb[t, 1], cv[1, :, s]).astype(BF16)

            @pl.when(has_next)
            def _():
                p_copy(t, h).start()

        pl.when(t == DEG)(lambda: gram_start(0, 0))

        acc[0] = mm(zb[t, 0], dv[0]) + mm(zb[t, 1], ct[0])
        acc[1] = mm(zb[t, 1], dv[1]) + mm(zb[t, 0], cv[0])

        pl.when(t == DEG)(lambda: reduce_middle(0))

        @pl.when(t == DEG + 1)
        def _():
            factors[0] = stacked_factor(cholesky_inverse(gram_end(0)))

        def update(l, s, total):
            now = zf[cur, l, :, s]
            value = (factor * inverse) * (total - centre * now) - back * zf[nxt, l, :, s]
            zf[nxt, l, :, s] = value
            zb[t + 1, l, :, s] = value.astype(BF16)

        pl.when(has_next)(lambda: z_copy(t, 0).wait_recv())
        acc[1] += mm(rz[t, :, columns[0]], ct[1, columns[0], :])
        pl.when(has_next)(lambda: z_copy(t, 1).wait_recv())
        everything = pl.ds(0, width)
        update(1, everything, acc[1] + mm(rz[t, :, columns[1]], ct[1, columns[1], :]))

        for h, s in enumerate(columns):
            pl.when(has_prev)(lambda: p_copy(t, h).wait_recv())
            update(0, s, acc[0, :, s] + rp[t, h].astype(F32))
        return carry

    runs = STEPS * DEG
    lax.fori_loop(0, runs, apply_step, 0)

    for l in range(2):
        value = mm(factors[0], stacked_rows(zf[0, l]))
        zf[0, l] = value
        ylow_out[l] = value[:EDGE].astype(BF16)

    below, above = {"cuts": cut - 1}, {"cuts": cut + 1}
    ylow_copy = remote(ylow_out, ylow_in, es.at[0], er.at[0], below)
    high_copy = remote(high_out, high_in, es.at[1], er.at[1], above)
    corr_copy = remote(corr_out, corr_in, es.at[2], er.at[2], above)
    pl.when(has_below)(ylow_copy.start)
    gram_start(1, 0)
    reduce_middle(1)

    pl.when(has_above)(ylow_copy.wait_recv)
    cross = jnp.zeros((k, EDGE), F32)
    corner = jnp.zeros((EDGE, EDGE), F32)
    for l in range(2):
        y_high, y_low = split(zf[0, l])
        cross = cross + mm(y_high, ylow_in[l], NT) + mm(y_low, ylow_in[l], NT)
        corner = corner + mm(ylow_in[l], ylow_in[l], NT)
    pieces = [cross[EDGE * i : EDGE * (i + 1)] for i in range(k // EDGE)] + [corner]
    pieces.append(jnp.zeros((EDGE, 128 - EDGE * len(pieces)), F32))
    packed = jnp.concatenate(pieces, axis=1)
    reduce_start(2, jnp.concatenate([packed, jnp.zeros((k // 2 - EDGE, 128), F32)], axis=0))
    reduce_middle(2)

    factor = cholesky_inverse(gram_end(1))
    factors[0] = stacked_factor(factor)
    factor_edge = factor[k - EDGE :]
    edge_rows = stacked_factor(factor_edge)
    for l in range(2):
        high_out[l] = mm(edge_rows, stacked_rows(zf[0, l])).astype(BF16)
    pl.when(has_above)(high_copy.start)
    for l in range(2):
        out[l] = mm(factors[0], stacked_rows(zf[0, l]))

    packed = reduce_end(2)[:EDGE] * scale
    cross = jnp.concatenate(
        [packed[:, EDGE * i : EDGE * (i + 1)] for i in range(k // EDGE)], axis=0
    )
    corner = packed[:, k : k + EDGE]
    rows_at = lax.broadcasted_iota(jnp.int32, (EDGE, EDGE), 0)
    lanes_at = lax.broadcasted_iota(jnp.int32, (EDGE, EDGE), 1)
    corner = jnp.where(has_above, corner, (rows_at == lanes_at).astype(F32))
    above_factor = cholesky_inverse(corner)
    corr = exact(exact(above_factor, cross, NT), factor_edge, NT)
    corr_out[...] = jnp.concatenate([corr, jnp.zeros((EDGE, 128 - EDGE), F32)], axis=1)
    pl.when(has_above)(corr_copy.start)

    f_high, f_low = split(above_factor)
    c_high, c_low = split(corr)
    for l in range(2):
        rows = mm(f_high, ylow_in[l]) + mm(f_low, ylow_in[l])
        r_high, r_low = split(rows)
        change = mm(c_high, r_high, TN) + mm(c_high, r_low, TN) + mm(c_low, r_high, TN)
        out[l, k - EDGE :, :] = out[l, k - EDGE :, :] - change

    pl.when(has_below)(high_copy.wait_recv)
    pl.when(has_below)(corr_copy.wait_recv)
    c_high, c_low = split(corr_in[:, :EDGE])
    for l in range(2):
        change = mm(c_high, high_in[l]) + mm(c_low, high_in[l])
        out[l, :EDGE, :] = out[l, :EDGE, :] - change

    pl.when(has_below)(ylow_copy.wait_send)
    pl.when(has_above)(high_copy.wait_send)
    pl.when(has_above)(corr_copy.wait_send)
    for i in range(3):
        for q in range(GROUP - 1):
            group_copy(i, q).wait_send()
        for q in range(n_z - 1):
            plane_copy(i, q).wait_send()

    def drain(t, carry):
        for h in range(2):
            pl.when(has_prev)(lambda: z_copy(t, h).wait_send())
            pl.when(has_next)(lambda: p_copy(t, h).wait_send())
        return carry

    lax.fori_loop(0, runs, drain, 0)


def per_device(sizes, vectors, diag_blocks, couplings, bounds):
    x = jnp.transpose(vectors[0], (1, 0, 2))
    _, k, width = x.shape
    n_z = sizes[1] // GROUP
    runs = STEPS * DEG
    vmem = pl.BlockSpec(memory_space=pltpu.VMEM)
    hbm = pl.BlockSpec(memory_space=pltpu.HBM)
    dma = pltpu.SemaphoreType.DMA
    result = pl.pallas_call(
        functools.partial(kernel, sizes),
        out_shape=jax.ShapeDtypeStruct(x.shape, F32),
        in_specs=[hbm, vmem, hbm, hbm],
        out_specs=vmem,
        scratch_shapes=[
            pltpu.SMEM((1, 2), jnp.int32),
            pltpu.VMEM((2, width, width), BF16),
            pltpu.VMEM((2, width, width), BF16),
            pltpu.VMEM((2, width, width), BF16),
            pltpu.VMEM((2, 2, k, width), F32),
            pltpu.VMEM((runs + 1, 2, k, width), BF16),
            pltpu.VMEM((runs, 2, k, width // 2), BF16),
            pltpu.VMEM((runs, k, width), BF16),
            pltpu.VMEM((runs, 2, k, width // 2), BF16),
            pltpu.VMEM((2, k, width), F32),
            pltpu.VMEM((3, 2, k // 2, 128), F32),
            pltpu.VMEM((3, GROUP - 1, k // 2, 128), F32),
            pltpu.VMEM((3, n_z - 1, k // 2, 128), F32),
            pltpu.VMEM((1, k, 3 * k), BF16),
            pltpu.VMEM((2, EDGE, width), BF16),
            pltpu.VMEM((2, EDGE, width), BF16),
            pltpu.VMEM((2, EDGE, width), BF16),
            pltpu.VMEM((2, EDGE, width), BF16),
            pltpu.VMEM((EDGE, 128), F32),
            pltpu.VMEM((EDGE, 128), F32),
            dma((5,)),
            dma((runs, 2)),
            dma((runs, 2)),
            dma((runs, 2)),
            dma((runs, 2)),
            dma((3, GROUP - 1)),
            dma((3, GROUP - 1)),
            dma((3, n_z - 1)),
            dma((3, n_z - 1)),
            dma((3,)),
            dma((3,)),
        ],
        compiler_params=pltpu.CompilerParams(
            collective_id=0, has_side_effects=True, vmem_limit_bytes=62 << 20
        ),
    )(bounds, x, diag_blocks, couplings)
    return jnp.transpose(result, (1, 0, 2))[None]


def solution(mesh):
    sizes = (mesh.shape["cuts"], mesh.shape["layer"])
    in_specs = (
        P("cuts", None, "layer", None),
        P("layer", None, None),
        P("layer", None, None),
        P("cuts", None),
    )
    return jax.shard_map(
        functools.partial(per_device, sizes),
        mesh=mesh,
        in_specs=in_specs,
        out_specs=P("cuts", None, "layer", None),
        check_vma=False,
    )
```

```python
import functools

import jax
import jax.numpy as jnp
from jax import lax
from jax.experimental import pallas as pl
from jax.experimental.pallas import tpu as pltpu
from jax.sharding import PartitionSpec as P

EDGE = 16
DEG = 4
STEPS = 2
GROUP = 4
F32 = jnp.float32
BF16 = jnp.bfloat16
NN = (((1,), (0,)), ((), ()))
NT = (((1,), (1,)), ((), ()))
TN = (((0,), (0,)), ((), ()))
MESH = pl.DeviceIdType.MESH


def mm(a, b, dims=NN):
    return lax.dot_general(a, b, dims, preferred_element_type=F32)


def split(value):
    high = value.astype(BF16)
    return high, (value - high.astype(F32)).astype(BF16)


def cholesky_inverse(gram, group=8):
    n = gram.shape[0]
    rows_at = lax.broadcasted_iota(jnp.int32, (n, n), 0)
    lanes_at = lax.broadcasted_iota(jnp.int32, (n, n), 1)
    eye = (rows_at == lanes_at).astype(F32)
    whole = jnp.concatenate([gram, eye], axis=1)
    shape = (8, 2 * n)
    blocks = [whole[8 * b : 8 * b + 8] for b in range(n // 8)]
    inner = lax.broadcasted_iota(jnp.int32, shape, 0)
    for j in range(0, n, group):
        home, at = j // 8, j % 8
        active = range(home, n // 8)
        rows = [jnp.broadcast_to(blocks[home][at + i : at + i + 1], shape) for i in range(group)]
        cross = {
            (i, m): jnp.broadcast_to(rows[i][:, j + m : j + m + 1], shape)
            for i in range(group)
            for m in range(i, group)
        }
        columns = {
            (b, i): jnp.broadcast_to(blocks[b][:, j + i : j + i + 1], shape)
            for b in active
            for i in range(group)
        }
        for i in range(group):
            inverse = 1.0 / cross[i, i]
            scaled = rows[i] * inverse
            later = range(i + 1, group)
            ratio = {m: cross[i, m] * inverse for m in later}
            for m in later:
                rows[m] = rows[m] - cross[i, m] * scaled
                for q in range(m, group):
                    cross[m, q] = cross[m, q] - cross[i, m] * ratio[q]
            for b in active:
                column = columns[b, i]
                for m in later:
                    columns[b, m] = columns[b, m] - column * ratio[m]
                if b == home:
                    column = jnp.where(inner > at + i, column, 0.0)
                blocks[b] = blocks[b] - column * scaled
    whole = jnp.concatenate(blocks, axis=0)
    diagonal = jnp.sum(whole[:, :n] * eye, axis=1, keepdims=True)
    return whole[:, n:] * lax.rsqrt(diagonal)


def stacked_factor(factor):
    high, low = split(factor)
    return jnp.concatenate([high, high, low], axis=1)


def stacked_rows(rows):
    high, low = split(rows)
    return jnp.concatenate([high, low, high], axis=0)


def exact(a, b, dims):
    return lax.dot_general(
        a, b, dims, precision=lax.Precision.HIGHEST, preferred_element_type=F32
    )


def kernel(
    sizes, bounds_hbm, x_in, d_hbm, c_hbm, out,
    bounds, x_own, dv, cv, ct, zf, zb, pb, rz, rp, acc, own, first, second, factors,
    ylow_out, ylow_in, high_out, high_in, corr_out, corr_in,
    load_sem, zs, zr, ps, pr, a1s, a1r, a2s, a2r, es, er, ready,
):
    n_cuts, n_layer = sizes
    n_z = n_layer // GROUP
    me = lax.axis_index("layer")
    cut = lax.axis_index("cuts")
    plane, member = me // GROUP, me % GROUP
    k, _, width = x_in.shape
    half = width // 2
    scale = 1.0 / (n_layer * 2 * width)
    has_prev, has_next = me > 0, me < n_layer - 1
    has_below, has_above = cut > 0, cut < n_cuts - 1
    group_peer = [plane * GROUP + (member + q) % GROUP for q in range(1, GROUP)]
    far_first = sorted(range(1, n_z), key=lambda q: -min(q, n_z - q))
    plane_peer = [((plane + q) % n_z) * GROUP + member for q in far_first]

    x_load = pltpu.make_async_copy(x_in, x_own, load_sem.at[5])
    x_load.start()
    bounds_load = pltpu.make_async_copy(bounds_hbm, bounds, load_sem.at[4])
    bounds_load.start()
    loads = []
    for i, (src, dst) in enumerate(((c_hbm, cv), (d_hbm, dv))):
        for l in (1, 0):
            loads.append(pltpu.make_async_copy(src.at[l], dst.at[l], load_sem.at[2 * i + l]))
    for copy in loads:
        copy.start()

    barrier = pltpu.get_barrier_semaphore()

    def ring(step):
        return {"layer": (me + step + n_layer) % n_layer}

    def greet(device):
        pl.semaphore_signal(barrier, inc=1, device_id=device, device_id_type=MESH)

    greet(ring(1))
    greet(ring(-1))
    pl.when(has_below)(lambda: greet({"cuts": cut - 1}))
    pl.when(has_above)(lambda: greet({"cuts": cut + 1}))

    for l in range(2):
        zf[1, l] = jnp.zeros((k, width), F32)

    @pl.when(jnp.logical_not(has_next))
    def _():
        rz[...] = jnp.zeros_like(rz)

    @pl.when(jnp.logical_not(has_prev))
    def _():
        rp[...] = jnp.zeros_like(rp)

    @pl.when(jnp.logical_not(has_below))
    def _():
        high_in[...] = jnp.zeros_like(high_in)
        corr_in[...] = jnp.zeros_like(corr_in)

    @pl.when(jnp.logical_not(has_above))
    def _():
        ylow_in[...] = jnp.zeros_like(ylow_in)

    bounds_load.wait()
    low = bounds[0, 0].astype(F32) / 64.0
    high = bounds[0, 1].astype(F32) / 64.0
    centre = jnp.full((8, 128), (low + high) / 2.0, F32)[:1, :1]
    inverse = 1.0 / jnp.full((8, 128), (high - low) / 2.0, F32)[:1, :1]
    x_load.wait()
    for l in range(2):
        mine = x_own[:, l, :]
        zf[0, l] = mine
        zb[0, l] = mine.astype(BF16)

    greeted = 2 + jnp.where(has_below, 1, 0) + jnp.where(has_above, 1, 0)
    pl.semaphore_wait(barrier, greeted)

    rounds = ready.shape[0]

    def tell(r):
        for step in (1 << r, -(1 << r)):
            pl.semaphore_signal(
                ready.at[r], inc=1, device_id=ring(step), device_id_type=MESH
            )

    def hear(r):
        pl.semaphore_wait(ready.at[r], 2)

    columns = [pl.ds(h * half, half) for h in range(2)]

    def remote(src, dst, send, recv, device):
        return pltpu.make_async_remote_copy(
            src, dst, send, recv, device_id=device, device_id_type=MESH
        )

    def z_copy(t, h):
        return remote(
            zb.at[t, 0, :, columns[h]], rz.at[t, :, columns[h]], zs.at[t, h], zr.at[t, h],
            {"layer": me - 1},
        )

    def p_copy(t, h):
        return remote(
            pb.at[t, h], rp.at[t, h], ps.at[t, h], pr.at[t, h], {"layer": me + 1}
        )

    lengths = [pl.ds(0, rows) for rows in (k // 2, k // 2, EDGE)]

    def group_copy(i, q):
        return remote(
            own.at[i, 0, lengths[i]], first.at[i, q, lengths[i]],
            a1s.at[i, q], a1r.at[i, q], {"layer": group_peer[q]},
        )

    def plane_copy(i, q):
        return remote(
            own.at[i, 1, lengths[i]], second.at[i, q, lengths[i]],
            a2s.at[i, q], a2r.at[i, q], {"layer": plane_peer[q]},
        )

    def reduce_start(i, value):
        own[i, 0, lengths[i]] = value
        for q in range(GROUP - 1):
            group_copy(i, q).start()

    def reduce_middle(i):
        for q in range(GROUP - 1):
            group_copy(i, q).wait_recv()
        total = own[i, 0, lengths[i]]
        for q in range(GROUP - 1):
            total = total + first[i, q, lengths[i]]
        own[i, 1, lengths[i]] = total
        for q in range(n_z - 1):
            plane_copy(i, q).start()

    def reduce_end(i):
        for q in range(n_z - 1):
            plane_copy(i, q).wait_recv()
        total = own[i, 1, lengths[i]]
        for q in range(n_z - 1):
            total = total + second[i, q, lengths[i]]
        return total

    def gram_start(i, src):
        gram = jnp.zeros((2 * k, 2 * k), F32)
        for l in range(2):
            pair = jnp.concatenate(split(zf[src, l]), axis=0)
            gram = gram + mm(pair, pair, NT)
        gram = gram[:k, :k] + gram[:k, k:] + gram[k:, :k]
        reduce_start(i, jnp.concatenate([gram[: k // 2], gram[k // 2 :]], axis=1))

    def gram_end(i):
        packed = reduce_end(i)
        return jnp.concatenate([packed[:, :k], packed[:, k:]], axis=0) * scale

    def apply_step(t, carry):
        cur, nxt = t % 2, (t + 1) % 2
        opening = t % DEG == 0
        factor, back = jnp.where(opening, 1.0, 2.0), jnp.where(opening, 0.0, 1.0)

        @pl.when(has_prev)
        def _():
            z_copy(t, 0).start()
            z_copy(t, 1).start()

        @pl.when(t == 0)
        def _():
            tell(0)
            loads[0].wait()

        for r in range(rounds):

            @pl.when(t == r + 1)
            def _():
                hear(r)
                if r + 1 < rounds:
                    tell(r + 1)

        for h, s in enumerate(columns):
            pb[t, h] = mm(zb[t, 1], cv[1, :, s]).astype(BF16)

            @pl.when(has_next)
            def _():
                p_copy(t, h).start()

        @pl.when(t == 0)
        def _():
            for copy in loads[1:]:
                copy.wait()
            for l in (1, 0):
                ct[l] = jnp.transpose(cv[l])

        pl.when(t == DEG)(lambda: gram_start(0, 0))
        pl.when(t == DEG + 1)(lambda: reduce_middle(0))

        acc[0] = mm(zb[t, 0], dv[0]) + mm(zb[t, 1], ct[0])
        acc[1] = mm(zb[t, 1], dv[1]) + mm(zb[t, 0], cv[0])

        @pl.when(t == 2 * DEG - 1)
        def _():
            factors[0] = stacked_factor(cholesky_inverse(gram_end(0)))

        def update(l, s, total):
            now = zf[cur, l, :, s]
            value = (factor * inverse) * (total - centre * now) - back * zf[nxt, l, :, s]
            zf[nxt, l, :, s] = value
            zb[t + 1, l, :, s] = value.astype(BF16)

        pl.when(has_next)(lambda: z_copy(t, 0).wait_recv())
        acc[1] += mm(rz[t, :, columns[0]], ct[1, columns[0], :])
        pl.when(has_next)(lambda: z_copy(t, 1).wait_recv())
        everything = pl.ds(0, width)
        update(1, everything, acc[1] + mm(rz[t, :, columns[1]], ct[1, columns[1], :]))

        for h, s in enumerate(columns):
            pl.when(has_prev)(lambda: p_copy(t, h).wait_recv())
            update(0, s, acc[0, :, s] + rp[t, h].astype(F32))
        return carry

    runs = STEPS * DEG
    lax.fori_loop(0, runs, apply_step, 0)

    for l in range(2):
        value = mm(factors[0], stacked_rows(zf[0, l]))
        zf[0, l] = value
        ylow_out[l] = value[:EDGE].astype(BF16)

    below, above = {"cuts": cut - 1}, {"cuts": cut + 1}
    ylow_copy = remote(ylow_out, ylow_in, es.at[0], er.at[0], below)
    high_copy = remote(high_out, high_in, es.at[1], er.at[1], above)
    corr_copy = remote(corr_out, corr_in, es.at[2], er.at[2], above)
    pl.when(has_below)(ylow_copy.start)
    gram_start(1, 0)
    reduce_middle(1)

    pl.when(has_above)(ylow_copy.wait_recv)
    cross = jnp.zeros((k, EDGE), F32)
    corner = jnp.zeros((EDGE, EDGE), F32)
    for l in range(2):
        y_high, y_low = split(zf[0, l])
        cross = cross + mm(y_high, ylow_in[l], NT) + mm(y_low, ylow_in[l], NT)
        corner = corner + mm(ylow_in[l], ylow_in[l], NT)
    pieces = [cross[EDGE * i : EDGE * (i + 1)] for i in range(k // EDGE)] + [corner]
    pieces.append(jnp.zeros((EDGE, 128 - EDGE * len(pieces)), F32))
    packed = jnp.concatenate(pieces, axis=1)
    reduce_start(2, packed)
    reduce_middle(2)

    factor = cholesky_inverse(gram_end(1))
    factors[0] = stacked_factor(factor)
    factor_edge = factor[k - EDGE :]
    edge_rows = stacked_factor(factor_edge)
    for l in range(2):
        high_out[l] = mm(edge_rows, stacked_rows(zf[0, l])).astype(BF16)
    pl.when(has_above)(high_copy.start)
    for l in range(2):
        zf[1, l] = mm(factors[0], stacked_rows(zf[0, l]))
        out[EDGE : k - EDGE, l, :] = zf[1, l, EDGE : k - EDGE]

    packed = reduce_end(2) * scale
    cross = jnp.concatenate(
        [packed[:, EDGE * i : EDGE * (i + 1)] for i in range(k // EDGE)], axis=0
    )
    corner = packed[:, k : k + EDGE]
    rows_at = lax.broadcasted_iota(jnp.int32, (EDGE, EDGE), 0)
    lanes_at = lax.broadcasted_iota(jnp.int32, (EDGE, EDGE), 1)
    corner = jnp.where(has_above, corner, (rows_at == lanes_at).astype(F32))
    above_factor = cholesky_inverse(corner)
    corr = exact(exact(above_factor, cross, NT), factor_edge, NT)
    corr_out[...] = jnp.concatenate([corr, jnp.zeros((EDGE, 128 - EDGE), F32)], axis=1)
    pl.when(has_above)(corr_copy.start)

    f_high, f_low = split(above_factor)
    c_high, c_low = split(corr)
    for l in range(2):
        rows = mm(f_high, ylow_in[l]) + mm(f_low, ylow_in[l])
        r_high, r_low = split(rows)
        change = mm(c_high, r_high, TN) + mm(c_high, r_low, TN) + mm(c_low, r_high, TN)
        out[k - EDGE :, l, :] = zf[1, l, k - EDGE :] - change

    pl.when(has_below)(high_copy.wait_recv)
    pl.when(has_below)(corr_copy.wait_recv)
    c_high, c_low = split(corr_in[:, :EDGE])
    for l in range(2):
        change = mm(c_high, high_in[l]) + mm(c_low, high_in[l])
        out[:EDGE, l, :] = zf[1, l, :EDGE] - change

    pl.when(has_below)(ylow_copy.wait_send)
    pl.when(has_above)(high_copy.wait_send)
    pl.when(has_above)(corr_copy.wait_send)
    for i in range(3):
        for q in range(GROUP - 1):
            group_copy(i, q).wait_send()
        for q in range(n_z - 1):
            plane_copy(i, q).wait_send()

    def drain(t, carry):
        for h in range(2):
            pl.when(has_prev)(lambda: z_copy(t, h).wait_send())
            pl.when(has_next)(lambda: p_copy(t, h).wait_send())
        return carry

    lax.fori_loop(0, runs, drain, 0)


def per_device(sizes, vectors, diag_blocks, couplings, bounds):
    x = vectors[0]
    k, _, width = x.shape
    n_z = sizes[1] // GROUP
    runs = STEPS * DEG
    rounds = (sizes[1] // 2).bit_length() - 1
    vmem = pl.BlockSpec(memory_space=pltpu.VMEM)
    hbm = pl.BlockSpec(memory_space=pltpu.HBM)
    dma = pltpu.SemaphoreType.DMA
    result = pl.pallas_call(
        functools.partial(kernel, sizes),
        out_shape=jax.ShapeDtypeStruct(x.shape, F32),
        in_specs=[hbm] * 4,
        out_specs=vmem,
        scratch_shapes=[
            pltpu.SMEM((1, 2), jnp.int32),
            pltpu.VMEM((k, 2, width), F32),
            pltpu.VMEM((2, width, width), BF16),
            pltpu.VMEM((2, width, width), BF16),
            pltpu.VMEM((2, width, width), BF16),
            pltpu.VMEM((2, 2, k, width), F32),
            pltpu.VMEM((runs + 1, 2, k, width), BF16),
            pltpu.VMEM((runs, 2, k, width // 2), BF16),
            pltpu.VMEM((runs, k, width), BF16),
            pltpu.VMEM((runs, 2, k, width // 2), BF16),
            pltpu.VMEM((2, k, width), F32),
            pltpu.VMEM((3, 2, k // 2, 128), F32),
            pltpu.VMEM((3, GROUP - 1, k // 2, 128), F32),
            pltpu.VMEM((3, n_z - 1, k // 2, 128), F32),
            pltpu.VMEM((1, k, 3 * k), BF16),
            pltpu.VMEM((2, EDGE, width), BF16),
            pltpu.VMEM((2, EDGE, width), BF16),
            pltpu.VMEM((2, EDGE, width), BF16),
            pltpu.VMEM((2, EDGE, width), BF16),
            pltpu.VMEM((EDGE, 128), F32),
            pltpu.VMEM((EDGE, 128), F32),
            dma((6,)),
            dma((runs, 2)),
            dma((runs, 2)),
            dma((runs, 2)),
            dma((runs, 2)),
            dma((3, GROUP - 1)),
            dma((3, GROUP - 1)),
            dma((3, n_z - 1)),
            dma((3, n_z - 1)),
            dma((3,)),
            dma((3,)),
            pltpu.SemaphoreType.REGULAR((rounds,)),
        ],
        compiler_params=pltpu.CompilerParams(
            collective_id=0, has_side_effects=True, vmem_limit_bytes=61 << 20
        ),
    )(bounds, x, diag_blocks, couplings)
    return result[None]


def solution(mesh):
    sizes = (mesh.shape["cuts"], mesh.shape["layer"])
    in_specs = (
        P("cuts", None, "layer", None),
        P("layer", None, None),
        P("layer", None, None),
        P("cuts", None),
    )
    return jax.shard_map(
        functools.partial(per_device, sizes),
        mesh=mesh,
        in_specs=in_specs,
        out_specs=P("cuts", None, "layer", None),
        check_vma=False,
    )
```

```python
import functools

import jax
import jax.numpy as jnp
from jax import lax
from jax.experimental import pallas as pl
from jax.experimental.pallas import tpu as pltpu
from jax.sharding import PartitionSpec as P

EDGE = 16
DEG = 4
STEPS = 2
PARTS = 4
GROUP = 4
F32 = jnp.float32
BF16 = jnp.bfloat16
NN = (((1,), (0,)), ((), ()))
NT = (((1,), (1,)), ((), ()))
TN = (((0,), (0,)), ((), ()))
MESH = pl.DeviceIdType.MESH


def mm(a, b, dims=NN):
    return lax.dot_general(a, b, dims, preferred_element_type=F32)


def split(value):
    high = value.astype(BF16)
    return high, (value - high.astype(F32)).astype(BF16)


def cholesky_inverse(gram, group=8):
    n = gram.shape[0]
    rows_at = lax.broadcasted_iota(jnp.int32, (n, n), 0)
    lanes_at = lax.broadcasted_iota(jnp.int32, (n, n), 1)
    eye = (rows_at == lanes_at).astype(F32)
    whole = jnp.concatenate([gram, eye], axis=1)
    shape = (8, 2 * n)
    blocks = [whole[8 * b : 8 * b + 8] for b in range(n // 8)]
    inner = lax.broadcasted_iota(jnp.int32, shape, 0)
    for j in range(0, n, group):
        home, at = j // 8, j % 8
        active = range(home, n // 8)
        rows = [jnp.broadcast_to(blocks[home][at + i : at + i + 1], shape) for i in range(group)]
        cross = {
            (i, m): jnp.broadcast_to(rows[i][:, j + m : j + m + 1], shape)
            for i in range(group)
            for m in range(i, group)
        }
        columns = {
            (b, i): jnp.broadcast_to(blocks[b][:, j + i : j + i + 1], shape)
            for b in active
            for i in range(group)
        }
        for i in range(group):
            inverse = 1.0 / cross[i, i]
            scaled = rows[i] * inverse
            later = range(i + 1, group)
            ratio = {m: cross[i, m] * inverse for m in later}
            for m in later:
                rows[m] = rows[m] - cross[i, m] * scaled
                for q in range(m, group):
                    cross[m, q] = cross[m, q] - cross[i, m] * ratio[q]
            for b in active:
                column = columns[b, i]
                for m in later:
                    columns[b, m] = columns[b, m] - column * ratio[m]
                if b == home:
                    column = jnp.where(inner > at + i, column, 0.0)
                blocks[b] = blocks[b] - column * scaled
    whole = jnp.concatenate(blocks, axis=0)
    diagonal = jnp.sum(whole[:, :n] * eye, axis=1, keepdims=True)
    return whole[:, n:] * lax.rsqrt(diagonal)


def stacked_factor(factor):
    high, low = split(factor)
    return jnp.concatenate([high, high, low], axis=1)


def stacked_rows(rows):
    high, low = split(rows)
    return jnp.concatenate([high, low, high], axis=0)


def pack_symmetric(gram):
    q = gram.shape[0] // 2
    quarters = (gram[:q, :q], gram[q:, :q], gram[q:, q:])
    cut = 3 * q // 4
    tail = jnp.concatenate([block[cut:] for block in quarters], axis=0)
    return jnp.concatenate([block[:cut] for block in quarters] + [tail], axis=1)


def unpack_symmetric(packed, k):
    q = k // 2
    rest = q // 4
    top, side, bottom = (
        jnp.concatenate(
            [packed[:, q * i : q * (i + 1)], packed[rest * i : rest * (i + 1), 3 * q :]], axis=0
        )
        for i in range(3)
    )
    upper = jnp.concatenate([top, jnp.transpose(side)], axis=1)
    return jnp.concatenate([upper, jnp.concatenate([side, bottom], axis=1)], axis=0)


def exact(a, b, dims):
    return lax.dot_general(
        a, b, dims, precision=lax.Precision.HIGHEST, preferred_element_type=F32
    )


def kernel(
    sizes, bounds_hbm, x_in, d_hbm, c_hbm, out,
    bounds, x_own, dv, cv, ct, zf, zb, pb, rz, rp, acc, own, first, second, factors, stack,
    ylow_out, ylow_in, high_out, high_in, corr_out, corr_in,
    load_sem, zs, zr, ps, pr, a1s, a1r, a2s, a2r, es, er, ready,
):
    n_cuts, n_layer = sizes
    n_z = n_layer // GROUP
    me = lax.axis_index("layer")
    cut = lax.axis_index("cuts")
    plane, member = me // GROUP, me % GROUP
    k, _, width = x_in.shape
    part = width // PARTS
    scale = 1.0 / (n_layer * 2 * width)
    has_prev, has_next = me > 0, me < n_layer - 1
    has_below, has_above = cut > 0, cut < n_cuts - 1
    group_peer = [plane * GROUP + (member + q) % GROUP for q in range(1, GROUP)]
    far_first = sorted(range(1, n_z), key=lambda q: -min(q, n_z - q))
    plane_peer = [((plane + q) % n_z) * GROUP + member for q in far_first]

    x_load = pltpu.make_async_copy(x_in, x_own, load_sem.at[5])
    x_load.start()
    bounds_load = pltpu.make_async_copy(bounds_hbm, bounds, load_sem.at[4])
    bounds_load.start()
    loads = []
    for i, (src, dst) in enumerate(((c_hbm, cv), (d_hbm, dv))):
        for l in (1, 0):
            loads.append(pltpu.make_async_copy(src.at[l], dst.at[l], load_sem.at[2 * i + l]))
    for copy in loads:
        copy.start()

    barrier = pltpu.get_barrier_semaphore()

    def ring(step):
        return {"layer": (me + step + n_layer) % n_layer}

    def greet(device):
        pl.semaphore_signal(barrier, inc=1, device_id=device, device_id_type=MESH)

    greet(ring(1))
    greet(ring(-1))
    pl.when(has_below)(lambda: greet({"cuts": cut - 1}))
    pl.when(has_above)(lambda: greet({"cuts": cut + 1}))

    for l in range(2):
        zf[1, l] = jnp.zeros((k, width), F32)

    @pl.when(jnp.logical_not(has_next))
    def _():
        rz[...] = jnp.zeros_like(rz)

    @pl.when(jnp.logical_not(has_prev))
    def _():
        rp[...] = jnp.zeros_like(rp)

    @pl.when(jnp.logical_not(has_below))
    def _():
        high_in[...] = jnp.zeros_like(high_in)
        corr_in[...] = jnp.zeros_like(corr_in)

    @pl.when(jnp.logical_not(has_above))
    def _():
        ylow_in[...] = jnp.zeros_like(ylow_in)

    bounds_load.wait()
    low = bounds[0, 0].astype(F32) / 64.0
    high = bounds[0, 1].astype(F32) / 64.0
    centre = jnp.full((8, 128), (low + high) / 2.0, F32)[:1, :1]
    inverse = 1.0 / jnp.full((8, 128), (high - low) / 2.0, F32)[:1, :1]
    x_load.wait()
    for l in range(2):
        mine = x_own[:, l, :]
        zf[0, l] = mine
        zb[0, l] = mine.astype(BF16)

    greeted = 2 + jnp.where(has_below, 1, 0) + jnp.where(has_above, 1, 0)
    pl.semaphore_wait(barrier, greeted)

    rounds = ready.shape[0]

    def tell(r):
        for step in (1 << r, -(1 << r)):
            pl.semaphore_signal(
                ready.at[r], inc=1, device_id=ring(step), device_id_type=MESH
            )

    def hear(r):
        pl.semaphore_wait(ready.at[r], 2)

    columns = [pl.ds(h * part, part) for h in range(PARTS)]

    def remote(src, dst, send, recv, device):
        return pltpu.make_async_remote_copy(
            src, dst, send, recv, device_id=device, device_id_type=MESH
        )

    def z_copy(t, h):
        return remote(
            zb.at[t, 0, :, columns[h]], rz.at[t, :, columns[h]], zs.at[t, h], zr.at[t, h],
            {"layer": me - 1},
        )

    def p_copy(t, h):
        return remote(
            pb.at[t, h], rp.at[t, h], ps.at[t, h], pr.at[t, h], {"layer": me + 1}
        )

    lengths = [pl.ds(0, rows) for rows in (3 * k // 8, 3 * k // 8, EDGE)]

    def group_copy(i, q):
        return remote(
            own.at[i, 0, lengths[i]], first.at[i, q, lengths[i]],
            a1s.at[i, q], a1r.at[i, q], {"layer": group_peer[q]},
        )

    def plane_copy(i, q):
        return remote(
            own.at[i, 1, lengths[i]], second.at[i, q, lengths[i]],
            a2s.at[i, q], a2r.at[i, q], {"layer": plane_peer[q]},
        )

    def reduce_start(i, value):
        own[i, 0, lengths[i]] = value
        for q in range(GROUP - 1):
            group_copy(i, q).start()

    def reduce_middle(i):
        for q in range(GROUP - 1):
            group_copy(i, q).wait_recv()
        total = own[i, 0, lengths[i]]
        for q in range(GROUP - 1):
            total = total + first[i, q, lengths[i]]
        own[i, 1, lengths[i]] = total
        for q in range(n_z - 1):
            plane_copy(i, q).start()

    def reduce_end(i):
        for q in range(n_z - 1):
            plane_copy(i, q).wait_recv()
        total = own[i, 1, lengths[i]]
        for q in range(n_z - 1):
            total = total + second[i, q, lengths[i]]
        return total

    def gram_start(i, pairs):
        gram = jnp.zeros((2 * k, 2 * k), F32)
        for pair in pairs:
            gram = gram + mm(pair, pair, NT)
        reduce_start(i, pack_symmetric(gram[:k, :k] + gram[:k, k:] + gram[k:, :k]))

    def gram_end(i):
        return unpack_symmetric(reduce_end(i), k) * scale

    def first_gram():
        gram_start(0, [jnp.concatenate(split(zf[0, l]), axis=0) for l in range(2)])

    runs = STEPS * DEG

    def send_product(t):
        for h, s in enumerate(columns):
            pb[t, h] = mm(zb[t, 1], cv[1, :, s]).astype(BF16)
            pl.when(has_next)(lambda: p_copy(t, h).start())

    def apply_step(t, carry):
        cur, nxt = t % 2, (t + 1) % 2
        opening = t % DEG == 0
        factor, back = jnp.where(opening, 1.0, 2.0), jnp.where(opening, 0.0, 1.0)
        more = t + 1 < runs

        for r in range(rounds):

            @pl.when(t == r + 1)
            def _():
                hear(r)
                if r + 1 < rounds:
                    tell(r + 1)

        pl.when(t == DEG)(first_gram)
        pl.when(t == DEG + 1)(lambda: reduce_middle(0))

        acc[0] = mm(zb[t, 0], dv[0]) + mm(zb[t, 1], ct[0])
        acc[1] = mm(zb[t, 1], dv[1]) + mm(zb[t, 0], cv[0])

        @pl.when(t == runs - 1)
        def _():
            factors[...] = stacked_factor(cholesky_inverse(gram_end(0)))

        def update(l, s, total):
            now = zf[cur, l, :, s]
            value = (factor * inverse) * (total - centre * now) - back * zf[nxt, l, :, s]
            zf[nxt, l, :, s] = value
            zb[t + 1, l, :, s] = value.astype(BF16)

        for h, s in enumerate(columns):
            pl.when(has_next)(lambda: z_copy(t, h).wait_recv())
            total = acc[1] + mm(rz[t, :, s], ct[1, s, :])
            if h + 1 < PARTS:
                acc[1] = total
            else:
                update(1, pl.ds(0, width), total)

        pl.when(more)(lambda: send_product(t + 1))

        for h, s in enumerate(columns):
            pl.when(has_prev)(lambda: p_copy(t, h).wait_recv())
            update(0, s, acc[0, :, s] + rp[t, h].astype(F32))
            pl.when(jnp.logical_and(has_prev, more))(lambda: z_copy(t + 1, h).start())
        return carry

    for h in range(PARTS):
        pl.when(has_prev)(lambda: z_copy(0, h).start())
    tell(0)
    loads[0].wait()
    send_product(0)
    for copy in loads[1:]:
        copy.wait()
    for l in (1, 0):
        ct[l] = jnp.transpose(cv[l])
    lax.fori_loop(0, runs, apply_step, 0)

    below, above = {"cuts": cut - 1}, {"cuts": cut + 1}
    ylow_copy = remote(ylow_out, ylow_in, es.at[0], er.at[0], below)
    cross_copy = remote(corr_out, corr_in, es.at[1], er.at[1], above)
    high_copies = [
        remote(high_out.at[l], high_in.at[l], es.at[2 + l], er.at[2 + l], above) for l in range(2)
    ]
    for l in range(2):
        stack[l] = stacked_rows(zf[0, l])
        ylow_out[l] = mm(factors[:EDGE], stack[l]).astype(BF16)
    pl.when(has_below)(ylow_copy.start)
    for l in range(2):
        stack[l] = stacked_rows(mm(factors[...], stack[l]))
    gram_start(1, [stack[l, : 2 * k] for l in range(2)])
    reduce_middle(1)

    pl.when(has_above)(ylow_copy.wait_recv)
    cross = jnp.zeros((EDGE, k), F32)
    corner = jnp.zeros((EDGE, EDGE), F32)
    for l in range(2):
        cross = cross + mm(ylow_in[l], stack[l, :k], NT) + mm(ylow_in[l], stack[l, k : 2 * k], NT)
        corner = corner + mm(ylow_in[l], ylow_in[l], NT)
    blank = jnp.zeros((EDGE, 128 - k - EDGE), F32)
    reduce_start(2, jnp.concatenate([cross, corner, blank], axis=1))
    reduce_middle(2)

    factor = cholesky_inverse(gram_end(1))
    factor_edge = factor[k - EDGE :]
    edge_rows = stacked_factor(factor_edge)
    for l in range(2):
        high_out[l] = mm(edge_rows, stack[l]).astype(BF16)
        pl.when(has_above)(high_copies[l].start)
    all_rows = stacked_factor(factor)
    for l in range(2):
        zf[1, l] = mm(all_rows, stack[l])
        out[EDGE : k - EDGE, l, :] = zf[1, l, EDGE : k - EDGE]

    packed = reduce_end(2) * scale
    projected = exact(packed[:, :k], factor_edge, NT)
    corr_out[...] = jnp.concatenate([projected, jnp.zeros((EDGE, 128 - EDGE), F32)], axis=1)
    pl.when(has_above)(cross_copy.start)

    corner = packed[:, k : k + EDGE]
    rows_at = lax.broadcasted_iota(jnp.int32, (EDGE, EDGE), 0)
    lanes_at = lax.broadcasted_iota(jnp.int32, (EDGE, EDGE), 1)
    corner = jnp.where(has_above, corner, (rows_at == lanes_at).astype(F32))
    above_factor = cholesky_inverse(corner)
    corr = exact(above_factor, projected, NN)
    w_high, w_low = split(exact(corr, above_factor, TN))
    for l in range(2):
        change = mm(w_high, ylow_in[l]) + mm(w_low, ylow_in[l])
        out[k - EDGE :, l, :] = zf[1, l, k - EDGE :] - change

    pl.when(has_below)(cross_copy.wait_recv)
    c_high, c_low = split(exact(factor[:EDGE, :EDGE], corr_in[:, :EDGE], NN))
    for l in range(2):
        pl.when(has_below)(high_copies[l].wait_recv)
        change = mm(c_high, high_in[l]) + mm(c_low, high_in[l])
        out[:EDGE, l, :] = zf[1, l, :EDGE] - change

    pl.when(has_below)(ylow_copy.wait_send)
    for copy in [cross_copy] + high_copies:
        pl.when(has_above)(copy.wait_send)
    for i in range(3):
        for q in range(GROUP - 1):
            group_copy(i, q).wait_send()
        for q in range(n_z - 1):
            plane_copy(i, q).wait_send()

    def drain(t, carry):
        for h in range(PARTS):
            pl.when(has_prev)(lambda: z_copy(t, h).wait_send())
            pl.when(has_next)(lambda: p_copy(t, h).wait_send())
        return carry

    lax.fori_loop(0, runs, drain, 0)


def per_device(sizes, vectors, diag_blocks, couplings, bounds):
    x = vectors[0]
    k, _, width = x.shape
    n_z = sizes[1] // GROUP
    runs = STEPS * DEG
    rounds = (sizes[1] // 2).bit_length() - 1
    vmem = pl.BlockSpec(memory_space=pltpu.VMEM)
    hbm = pl.BlockSpec(memory_space=pltpu.HBM)
    dma = pltpu.SemaphoreType.DMA
    result = pl.pallas_call(
        functools.partial(kernel, sizes),
        out_shape=jax.ShapeDtypeStruct(x.shape, F32),
        in_specs=[hbm] * 4,
        out_specs=vmem,
        scratch_shapes=[
            pltpu.SMEM((1, 2), jnp.int32),
            pltpu.VMEM((k, 2, width), F32),
            pltpu.VMEM((2, width, width), BF16),
            pltpu.VMEM((2, width, width), BF16),
            pltpu.VMEM((2, width, width), BF16),
            pltpu.VMEM((2, 2, k, width), F32),
            pltpu.VMEM((runs + 1, 2, k, width), BF16),
            pltpu.VMEM((runs, PARTS, k, width // PARTS), BF16),
            pltpu.VMEM((runs, k, width), BF16),
            pltpu.VMEM((runs, PARTS, k, width // PARTS), BF16),
            pltpu.VMEM((2, k, width), F32),
            pltpu.VMEM((3, 2, 3 * k // 8, 128), F32),
            pltpu.VMEM((3, GROUP - 1, 3 * k // 8, 128), F32),
            pltpu.VMEM((3, n_z - 1, 3 * k // 8, 128), F32),
            pltpu.VMEM((k, 3 * k), BF16),
            pltpu.VMEM((2, 3 * k, width), BF16),
            pltpu.VMEM((2, EDGE, width), BF16),
            pltpu.VMEM((2, EDGE, width), BF16),
            pltpu.VMEM((2, EDGE, width), BF16),
            pltpu.VMEM((2, EDGE, width), BF16),
            pltpu.VMEM((EDGE, 128), F32),
            pltpu.VMEM((EDGE, 128), F32),
            dma((6,)),
            dma((runs, PARTS)),
            dma((runs, PARTS)),
            dma((runs, PARTS)),
            dma((runs, PARTS)),
            dma((3, GROUP - 1)),
            dma((3, GROUP - 1)),
            dma((3, n_z - 1)),
            dma((3, n_z - 1)),
            dma((4,)),
            dma((4,)),
            pltpu.SemaphoreType.REGULAR((rounds,)),
        ],
        compiler_params=pltpu.CompilerParams(
            collective_id=0, has_side_effects=True, vmem_limit_bytes=61 << 20
        ),
    )(bounds, x, diag_blocks, couplings)
    return result[None]


def solution(mesh):
    sizes = (mesh.shape["cuts"], mesh.shape["layer"])
    in_specs = (
        P("cuts", None, "layer", None),
        P("layer", None, None),
        P("layer", None, None),
        P("cuts", None),
    )
    return jax.shard_map(
        functools.partial(per_device, sizes),
        mesh=mesh,
        in_specs=in_specs,
        out_specs=P("cuts", None, "layer", None),
        check_vma=False,
    )
```

```python
import functools

import jax
import jax.numpy as jnp
from jax import lax
from jax.experimental import pallas as pl
from jax.experimental.pallas import tpu as pltpu
from jax.sharding import PartitionSpec as P

EDGE = 16
DEG = 4
STEPS = 2
PARTS = 4
GROUP = 4
F32 = jnp.float32
BF16 = jnp.bfloat16
NN = (((1,), (0,)), ((), ()))
NT = (((1,), (1,)), ((), ()))
TN = (((0,), (0,)), ((), ()))
MESH = pl.DeviceIdType.MESH


def mm(a, b, dims=NN):
    return lax.dot_general(a, b, dims, preferred_element_type=F32)


def split(value):
    high = value.astype(BF16)
    return high, (value - high.astype(F32)).astype(BF16)


def cholesky_inverse(gram, group=8):
    n = gram.shape[0]
    rows_at = lax.broadcasted_iota(jnp.int32, (n, n), 0)
    lanes_at = lax.broadcasted_iota(jnp.int32, (n, n), 1)
    eye = (rows_at == lanes_at).astype(F32)
    whole = jnp.concatenate([gram, eye], axis=1)
    shape = (8, 2 * n)
    blocks = [whole[8 * b : 8 * b + 8] for b in range(n // 8)]
    inner = lax.broadcasted_iota(jnp.int32, shape, 0)
    for j in range(0, n, group):
        home, at = j // 8, j % 8
        active = range(home, n // 8)
        rows = [jnp.broadcast_to(blocks[home][at + i : at + i + 1], shape) for i in range(group)]
        cross = {
            (i, m): jnp.broadcast_to(rows[i][:, j + m : j + m + 1], shape)
            for i in range(group)
            for m in range(i, group)
        }
        columns = {
            (b, i): jnp.broadcast_to(blocks[b][:, j + i : j + i + 1], shape)
            for b in active
            for i in range(group)
        }
        for i in range(group):
            inverse = 1.0 / cross[i, i]
            scaled = rows[i] * inverse
            later = range(i + 1, group)
            ratio = {m: cross[i, m] * inverse for m in later}
            for m in later:
                rows[m] = rows[m] - cross[i, m] * scaled
                for q in range(m, group):
                    cross[m, q] = cross[m, q] - cross[i, m] * ratio[q]
            for b in active:
                column = columns[b, i]
                for m in later:
                    columns[b, m] = columns[b, m] - column * ratio[m]
                if b == home:
                    column = jnp.where(inner > at + i, column, 0.0)
                blocks[b] = blocks[b] - column * scaled
    whole = jnp.concatenate(blocks, axis=0)
    diagonal = jnp.sum(whole[:, :n] * eye, axis=1, keepdims=True)
    return whole[:, n:] * lax.rsqrt(diagonal)


def stacked_factor(factor):
    high, low = split(factor)
    return jnp.concatenate([high, high, low], axis=1)


def stacked_rows(rows):
    high, low = split(rows)
    return jnp.concatenate([high, low, high], axis=0)


def pack_symmetric(gram):
    q = gram.shape[0] // 2
    quarters = (gram[:q, :q], gram[q:, :q], gram[q:, q:])
    cut = 3 * q // 4
    tail = jnp.concatenate([block[cut:] for block in quarters], axis=0)
    return jnp.concatenate([block[:cut] for block in quarters] + [tail], axis=1)


def unpack_symmetric(packed, k):
    q = k // 2
    rest = q // 4
    top, side, bottom = (
        jnp.concatenate(
            [packed[:, q * i : q * (i + 1)], packed[rest * i : rest * (i + 1), 3 * q :]], axis=0
        )
        for i in range(3)
    )
    upper = jnp.concatenate([top, jnp.transpose(side)], axis=1)
    return jnp.concatenate([upper, jnp.concatenate([side, bottom], axis=1)], axis=0)


def exact(a, b, dims):
    return lax.dot_general(
        a, b, dims, precision=lax.Precision.HIGHEST, preferred_element_type=F32
    )


def kernel(
    sizes, bounds_hbm, x_in, d_hbm, c_hbm, out,
    bounds, x_own, dv, cv, ct, zf, zb, pb, rz, rp, acc, own, first, second, factors, stack,
    ylow_out, ylow_in, high_out, high_in, tail_out, tail_in, cross_in,
    load_sem, zs, zr, ps, pr, a1s, a1r, a2s, a2r, es, er, xs, xr, ready,
):
    n_cuts, n_layer = sizes
    n_z = n_layer // GROUP
    me = lax.axis_index("layer")
    cut = lax.axis_index("cuts")
    plane, member = me // GROUP, me % GROUP
    k, _, width = x_in.shape
    part = width // PARTS
    scale = 1.0 / (n_layer * 2 * width)
    has_prev, has_next = me > 0, me < n_layer - 1
    has_below, has_above = cut > 0, cut < n_cuts - 1
    group_peer = [plane * GROUP + (member + q) % GROUP for q in range(1, GROUP)]
    far_first = sorted(range(1, n_z), key=lambda q: -min(q, n_z - q))
    plane_peer = [((plane + q) % n_z) * GROUP + member for q in far_first]

    x_load = pltpu.make_async_copy(x_in, x_own, load_sem.at[5])
    x_load.start()
    bounds_load = pltpu.make_async_copy(bounds_hbm, bounds, load_sem.at[4])
    bounds_load.start()
    loads = []
    for i, (src, dst) in enumerate(((c_hbm, cv), (d_hbm, dv))):
        for l in (1, 0):
            loads.append(pltpu.make_async_copy(src.at[l], dst.at[l], load_sem.at[2 * i + l]))
    for copy in loads:
        copy.start()

    barrier = pltpu.get_barrier_semaphore()

    def ring(step):
        return {"layer": (me + step + n_layer) % n_layer}

    def greet(device):
        pl.semaphore_signal(barrier, inc=1, device_id=device, device_id_type=MESH)

    greet(ring(1))
    greet(ring(-1))
    pl.when(has_below)(lambda: greet({"cuts": cut - 1}))
    pl.when(has_above)(lambda: greet({"cuts": cut + 1}))

    for l in range(2):
        zf[1, l] = jnp.zeros((k, width), F32)

    @pl.when(jnp.logical_not(has_next))
    def _():
        rz[...] = jnp.zeros_like(rz)

    @pl.when(jnp.logical_not(has_prev))
    def _():
        rp[...] = jnp.zeros_like(rp)

    @pl.when(jnp.logical_not(has_below))
    def _():
        high_in[...] = jnp.zeros_like(high_in)
        tail_in[...] = jnp.zeros_like(tail_in)
        cross_in[...] = jnp.zeros_like(cross_in)

    @pl.when(jnp.logical_not(has_above))
    def _():
        ylow_in[...] = jnp.zeros_like(ylow_in)

    bounds_load.wait()
    low = bounds[0, 0].astype(F32) / 64.0
    high = bounds[0, 1].astype(F32) / 64.0
    centre = jnp.full((8, 128), (low + high) / 2.0, F32)[:1, :1]
    inverse = 1.0 / jnp.full((8, 128), (high - low) / 2.0, F32)[:1, :1]
    x_load.wait()
    for l in range(2):
        mine = x_own[:, l, :]
        zf[0, l] = mine
        zb[0, l] = mine.astype(BF16)

    greeted = 2 + jnp.where(has_below, 1, 0) + jnp.where(has_above, 1, 0)
    pl.semaphore_wait(barrier, greeted)

    rounds = ready.shape[0]

    def tell(r):
        for step in (1 << r, -(1 << r)):
            pl.semaphore_signal(
                ready.at[r], inc=1, device_id=ring(step), device_id_type=MESH
            )

    def hear(r):
        pl.semaphore_wait(ready.at[r], 2)

    columns = [pl.ds(h * part, part) for h in range(PARTS)]

    def remote(src, dst, send, recv, device):
        return pltpu.make_async_remote_copy(
            src, dst, send, recv, device_id=device, device_id_type=MESH
        )

    def z_copy(t, h):
        return remote(
            zb.at[t, 0, :, columns[h]], rz.at[t, :, columns[h]], zs.at[t, h], zr.at[t, h],
            {"layer": me - 1},
        )

    def p_copy(t, h):
        return remote(
            pb.at[t, h], rp.at[t, h], ps.at[t, h], pr.at[t, h], {"layer": me + 1}
        )

    lengths = [pl.ds(0, rows) for rows in (3 * k // 8, 3 * k // 8, EDGE)]

    def group_copy(i, q):
        return remote(
            own.at[i, 0, lengths[i]], first.at[i, q, lengths[i]],
            a1s.at[i, q], a1r.at[i, q], {"layer": group_peer[q]},
        )

    def plane_copy(i, q):
        return remote(
            own.at[i, 1, lengths[i]], second.at[i, q, lengths[i]],
            a2s.at[i, q], a2r.at[i, q], {"layer": plane_peer[q]},
        )

    def reduce_start(i, value):
        own[i, 0, lengths[i]] = value
        for q in range(GROUP - 1):
            group_copy(i, q).start()

    def reduce_middle(i):
        for q in range(GROUP - 1):
            group_copy(i, q).wait_recv()
        total = own[i, 0, lengths[i]]
        for q in range(GROUP - 1):
            total = total + first[i, q, lengths[i]]
        own[i, 1, lengths[i]] = total
        for q in range(n_z - 1):
            plane_copy(i, q).start()

    def reduce_end(i):
        for q in range(n_z - 1):
            plane_copy(i, q).wait_recv()
        total = own[i, 1, lengths[i]]
        for q in range(n_z - 1):
            total = total + second[i, q, lengths[i]]
        return total

    def gram_start(i, pairs):
        gram = jnp.zeros((2 * k, 2 * k), F32)
        for pair in pairs:
            gram = gram + mm(pair, pair, NT)
        reduce_start(i, pack_symmetric(gram[:k, :k] + gram[:k, k:] + gram[k:, :k]))

    def gram_end(i):
        return unpack_symmetric(reduce_end(i), k) * scale

    def first_gram():
        gram_start(0, [jnp.concatenate(split(zf[0, l]), axis=0) for l in range(2)])

    runs = STEPS * DEG

    def send_product(t):
        for h, s in enumerate(columns):
            pb[t, h] = mm(zb[t, 1], cv[1, :, s]).astype(BF16)
            pl.when(has_next)(lambda: p_copy(t, h).start())

    def apply_step(t, carry):
        cur, nxt = t % 2, (t + 1) % 2
        opening = t % DEG == 0
        factor, back = jnp.where(opening, 1.0, 2.0), jnp.where(opening, 0.0, 1.0)
        more = t + 1 < runs

        for r in range(rounds):

            @pl.when(t == r + 1)
            def _():
                hear(r)
                if r + 1 < rounds:
                    tell(r + 1)

        pl.when(t == DEG)(first_gram)
        pl.when(t == DEG + 1)(lambda: reduce_middle(0))

        acc[0] = mm(zb[t, 0], dv[0]) + mm(zb[t, 1], ct[0])
        acc[1] = mm(zb[t, 1], dv[1]) + mm(zb[t, 0], cv[0])

        @pl.when(t == runs - 1)
        def _():
            factors[...] = stacked_factor(cholesky_inverse(gram_end(0)))

        def update(l, s, total):
            now = zf[cur, l, :, s]
            value = (factor * inverse) * (total - centre * now) - back * zf[nxt, l, :, s]
            zf[nxt, l, :, s] = value
            zb[t + 1, l, :, s] = value.astype(BF16)

        for h, s in enumerate(columns):
            pl.when(has_next)(lambda: z_copy(t, h).wait_recv())
            total = acc[1] + mm(rz[t, :, s], ct[1, s, :])
            if h + 1 < PARTS:
                acc[1] = total
            else:
                update(1, pl.ds(0, width), total)

        pl.when(more)(lambda: send_product(t + 1))

        for h, s in enumerate(columns):
            pl.when(has_prev)(lambda: p_copy(t, h).wait_recv())
            update(0, s, acc[0, :, s] + rp[t, h].astype(F32))
            pl.when(jnp.logical_and(has_prev, more))(lambda: z_copy(t + 1, h).start())
        return carry

    for h in range(PARTS):
        pl.when(has_prev)(lambda: z_copy(0, h).start())
    tell(0)
    loads[0].wait()
    send_product(0)
    for copy in loads[1:]:
        copy.wait()
    for l in (1, 0):
        ct[l] = jnp.transpose(cv[l])
    lax.fori_loop(0, runs, apply_step, 0)

    below, above = {"cuts": cut - 1}, {"cuts": cut + 1}
    ylow_copy = remote(ylow_out, ylow_in, es.at[0], er.at[0], below)
    tail_copy = remote(tail_out, tail_in, es.at[1], er.at[1], above)
    cross_copies = [
        remote(
            own.at[2, 1, lengths[2]], cross_in.at[q], xs.at[q], xr.at[q],
            {"cuts": cut + 1, "layer": ((plane + q) % n_z) * GROUP + member},
        )
        for q in far_first + [0]
    ]
    high_copies = [
        remote(high_out.at[l], high_in.at[l], es.at[2 + l], er.at[2 + l], above) for l in range(2)
    ]
    for l in range(2):
        stack[l] = stacked_rows(zf[0, l])
        ylow_out[l] = mm(factors[:EDGE], stack[l]).astype(BF16)
    pl.when(has_below)(ylow_copy.start)
    for l in range(2):
        stack[l] = stacked_rows(mm(factors[...], stack[l]))
    gram_start(1, [stack[l, : 2 * k] for l in range(2)])
    reduce_middle(1)

    pl.when(has_above)(ylow_copy.wait_recv)
    cross = jnp.zeros((EDGE, k), F32)
    corner = jnp.zeros((EDGE, EDGE), F32)
    for l in range(2):
        cross = cross + mm(ylow_in[l], stack[l, :k], NT) + mm(ylow_in[l], stack[l, k : 2 * k], NT)
        corner = corner + mm(ylow_in[l], ylow_in[l], NT)
    blank = jnp.zeros((EDGE, 128 - k - EDGE), F32)
    reduce_start(2, jnp.concatenate([cross, corner, blank], axis=1))
    reduce_middle(2)

    @pl.when(has_above)
    def _():
        for copy in cross_copies:
            copy.start()

    factor = cholesky_inverse(gram_end(1))
    factor_edge = factor[k - EDGE :]
    edge_rows = stacked_factor(factor_edge)
    tail_out[...] = jnp.concatenate([factor_edge, jnp.zeros((EDGE, 128 - k), F32)], axis=1)
    pl.when(has_above)(tail_copy.start)
    for l in range(2):
        high_out[l] = mm(edge_rows, stack[l]).astype(BF16)
        pl.when(has_above)(high_copies[l].start)
    all_rows = stacked_factor(factor)
    for l in range(2):
        zf[1, l] = mm(all_rows, stack[l])
        out[EDGE : k - EDGE, l, :] = zf[1, l, EDGE : k - EDGE]

    packed = reduce_end(2) * scale
    projected = exact(packed[:, :k], factor_edge, NT)
    corner = packed[:, k : k + EDGE]
    rows_at = lax.broadcasted_iota(jnp.int32, (EDGE, EDGE), 0)
    lanes_at = lax.broadcasted_iota(jnp.int32, (EDGE, EDGE), 1)
    corner = jnp.where(has_above, corner, (rows_at == lanes_at).astype(F32))
    above_factor = cholesky_inverse(corner)
    corr = exact(above_factor, projected, NN)
    w_high, w_low = split(exact(corr, above_factor, TN))
    for l in range(2):
        change = mm(w_high, ylow_in[l]) + mm(w_low, ylow_in[l])
        out[k - EDGE :, l, :] = zf[1, l, k - EDGE :] - change

    @pl.when(has_below)
    def _():
        tail_copy.wait_recv()
        for copy in cross_copies:
            copy.wait_recv()

    cross = cross_in[0]
    for q in range(1, n_z):
        cross = cross + cross_in[q]
    projected = exact(cross[:, :k] * scale, tail_in[:, :k], NT)
    c_high, c_low = split(exact(factor[:EDGE, :EDGE], projected, NN))
    for l in range(2):
        pl.when(has_below)(high_copies[l].wait_recv)
        change = mm(c_high, high_in[l]) + mm(c_low, high_in[l])
        out[:EDGE, l, :] = zf[1, l, :EDGE] - change

    pl.when(has_below)(ylow_copy.wait_send)
    for copy in [tail_copy] + high_copies + cross_copies:
        pl.when(has_above)(copy.wait_send)
    for i in range(3):
        for q in range(GROUP - 1):
            group_copy(i, q).wait_send()
        for q in range(n_z - 1):
            plane_copy(i, q).wait_send()

    def drain(t, carry):
        for h in range(PARTS):
            pl.when(has_prev)(lambda: z_copy(t, h).wait_send())
            pl.when(has_next)(lambda: p_copy(t, h).wait_send())
        return carry

    lax.fori_loop(0, runs, drain, 0)


def per_device(sizes, vectors, diag_blocks, couplings, bounds):
    x = vectors[0]
    k, _, width = x.shape
    n_z = sizes[1] // GROUP
    runs = STEPS * DEG
    rounds = (sizes[1] // 2).bit_length() - 1
    vmem = pl.BlockSpec(memory_space=pltpu.VMEM)
    hbm = pl.BlockSpec(memory_space=pltpu.HBM)
    dma = pltpu.SemaphoreType.DMA
    result = pl.pallas_call(
        functools.partial(kernel, sizes),
        out_shape=jax.ShapeDtypeStruct(x.shape, F32),
        in_specs=[hbm] * 4,
        out_specs=vmem,
        scratch_shapes=[
            pltpu.SMEM((1, 2), jnp.int32),
            pltpu.VMEM((k, 2, width), F32),
            pltpu.VMEM((2, width, width), BF16),
            pltpu.VMEM((2, width, width), BF16),
            pltpu.VMEM((2, width, width), BF16),
            pltpu.VMEM((2, 2, k, width), F32),
            pltpu.VMEM((runs + 1, 2, k, width), BF16),
            pltpu.VMEM((runs, PARTS, k, width // PARTS), BF16),
            pltpu.VMEM((runs, k, width), BF16),
            pltpu.VMEM((runs, PARTS, k, width // PARTS), BF16),
            pltpu.VMEM((2, k, width), F32),
            pltpu.VMEM((3, 2, 3 * k // 8, 128), F32),
            pltpu.VMEM((3, GROUP - 1, 3 * k // 8, 128), F32),
            pltpu.VMEM((3, n_z - 1, 3 * k // 8, 128), F32),
            pltpu.VMEM((k, 3 * k), BF16),
            pltpu.VMEM((2, 3 * k, width), BF16),
            pltpu.VMEM((2, EDGE, width), BF16),
            pltpu.VMEM((2, EDGE, width), BF16),
            pltpu.VMEM((2, EDGE, width), BF16),
            pltpu.VMEM((2, EDGE, width), BF16),
            pltpu.VMEM((EDGE, 128), F32),
            pltpu.VMEM((EDGE, 128), F32),
            pltpu.VMEM((n_z, EDGE, 128), F32),
            dma((6,)),
            dma((runs, PARTS)),
            dma((runs, PARTS)),
            dma((runs, PARTS)),
            dma((runs, PARTS)),
            dma((3, GROUP - 1)),
            dma((3, GROUP - 1)),
            dma((3, n_z - 1)),
            dma((3, n_z - 1)),
            dma((4,)),
            dma((4,)),
            dma((n_z,)),
            dma((n_z,)),
            pltpu.SemaphoreType.REGULAR((rounds,)),
        ],
        compiler_params=pltpu.CompilerParams(
            collective_id=0, has_side_effects=True, vmem_limit_bytes=48 << 20
        ),
    )(*(
        pltpu.with_memory_space_constraint(operand, pltpu.HBM)
        for operand in (bounds, x, diag_blocks, couplings)
    ))
    return result[None]


def solution(mesh):
    sizes = (mesh.shape["cuts"], mesh.shape["layer"])
    in_specs = (
        P("cuts", None, "layer", None),
        P("layer", None, None),
        P("layer", None, None),
        P("cuts", None),
    )
    return jax.shard_map(
        functools.partial(per_device, sizes),
        mesh=mesh,
        in_specs=in_specs,
        out_specs=P("cuts", None, "layer", None),
        check_vma=False,
    )
```

```python
import functools

import jax
import jax.numpy as jnp
from jax import lax
from jax.experimental import pallas as pl
from jax.experimental.pallas import tpu as pltpu
from jax.sharding import PartitionSpec as P

EDGE = 16
DEG = 4
STEPS = 2
PARTS = 4
GROUP = 4
F32 = jnp.float32
BF16 = jnp.bfloat16
NN = (((1,), (0,)), ((), ()))
NT = (((1,), (1,)), ((), ()))
TN = (((0,), (0,)), ((), ()))
MESH = pl.DeviceIdType.MESH


def mm(a, b, dims=NN):
    return lax.dot_general(a, b, dims, preferred_element_type=F32)


def split(value):
    high = value.astype(BF16)
    return high, (value - high.astype(F32)).astype(BF16)


def cholesky_inverse(gram, group=8):
    n = gram.shape[0]
    rows_at = lax.broadcasted_iota(jnp.int32, (n, n), 0)
    lanes_at = lax.broadcasted_iota(jnp.int32, (n, n), 1)
    eye = (rows_at == lanes_at).astype(F32)
    whole = jnp.concatenate([gram, eye], axis=1)
    shape = (8, 2 * n)
    blocks = [whole[8 * b : 8 * b + 8] for b in range(n // 8)]
    inner = lax.broadcasted_iota(jnp.int32, shape, 0)
    for j in range(0, n, group):
        home, at = j // 8, j % 8
        active = range(home, n // 8)
        rows = [jnp.broadcast_to(blocks[home][at + i : at + i + 1], shape) for i in range(group)]
        cross = {
            (i, m): jnp.broadcast_to(rows[i][:, j + m : j + m + 1], shape)
            for i in range(group)
            for m in range(i, group)
        }
        columns = {
            (b, i): jnp.broadcast_to(blocks[b][:, j + i : j + i + 1], shape)
            for b in active
            for i in range(group)
        }
        for i in range(group):
            inverse = 1.0 / cross[i, i]
            scaled = rows[i] * inverse
            later = range(i + 1, group)
            ratio = {m: cross[i, m] * inverse for m in later}
            for m in later:
                rows[m] = rows[m] - cross[i, m] * scaled
                for q in range(m, group):
                    cross[m, q] = cross[m, q] - cross[i, m] * ratio[q]
            for b in active:
                column = columns[b, i]
                for m in later:
                    columns[b, m] = columns[b, m] - column * ratio[m]
                if b == home:
                    column = jnp.where(inner > at + i, column, 0.0)
                blocks[b] = blocks[b] - column * scaled
    whole = jnp.concatenate(blocks, axis=0)
    diagonal = jnp.sum(whole[:, :n] * eye, axis=1, keepdims=True)
    return whole[:, n:] * lax.rsqrt(diagonal)


def stacked_factor(factor):
    high, low = split(factor)
    return jnp.concatenate([high, high, low], axis=1)


def stacked_rows(rows):
    high, low = split(rows)
    return jnp.concatenate([high, low, high], axis=0)


def pack_symmetric(gram):
    q = gram.shape[0] // 2
    quarters = (gram[:q, :q], gram[q:, :q], gram[q:, q:])
    cut = 3 * q // 4
    tail = jnp.concatenate([block[cut:] for block in quarters], axis=0)
    return jnp.concatenate([block[:cut] for block in quarters] + [tail], axis=1)


def unpack_symmetric(packed, k):
    q = k // 2
    rest = q // 4
    top, side, bottom = (
        jnp.concatenate(
            [packed[:, q * i : q * (i + 1)], packed[rest * i : rest * (i + 1), 3 * q :]], axis=0
        )
        for i in range(3)
    )
    upper = jnp.concatenate([top, jnp.transpose(side)], axis=1)
    return jnp.concatenate([upper, jnp.concatenate([side, bottom], axis=1)], axis=0)


def exact(a, b, dims):
    return lax.dot_general(
        a, b, dims, precision=lax.Precision.HIGHEST, preferred_element_type=F32
    )


def kernel(
    sizes, bounds_hbm, x_in, d_hbm, c_hbm, out,
    bounds, x_own, dv, cv, ct, zf, zb, pb, rz, rp, acc, own, first, second, factors, stack, gram_part, gram_first,
    ylow_out, ylow_in, high_out, high_in, tail_out, tail_in, cross_in,
    load_sem, zs, zr, ps, pr, a1s, a1r, a2s, a2r, es, er, xs, xr, ready,
):
    n_cuts, n_layer = sizes
    n_z = n_layer // GROUP
    me = lax.axis_index("layer")
    cut = lax.axis_index("cuts")
    plane, member = me // GROUP, me % GROUP
    k, _, width = x_in.shape
    part = width // PARTS
    scale = 1.0 / (n_layer * 2 * width)
    has_prev, has_next = me > 0, me < n_layer - 1
    has_below, has_above = cut > 0, cut < n_cuts - 1
    group_peer = [plane * GROUP + (member + q) % GROUP for q in range(1, GROUP)]
    far_first = sorted(range(1, n_z), key=lambda q: -min(q, n_z - q))
    plane_peer = [((plane + q) % n_z) * GROUP + member for q in far_first]

    x_load = pltpu.make_async_copy(x_in, x_own, load_sem.at[5])
    x_load.start()
    bounds_load = pltpu.make_async_copy(bounds_hbm, bounds, load_sem.at[4])
    bounds_load.start()
    loads = []
    for i, (src, dst) in enumerate(((c_hbm, cv), (d_hbm, dv))):
        for l in (1, 0):
            loads.append(pltpu.make_async_copy(src.at[l], dst.at[l], load_sem.at[2 * i + l]))
    for copy in loads:
        copy.start()

    barrier = pltpu.get_barrier_semaphore()

    def ring(step):
        return {"layer": (me + step + n_layer) % n_layer}

    def greet(device):
        pl.semaphore_signal(barrier, inc=1, device_id=device, device_id_type=MESH)

    greet(ring(1))
    greet(ring(-1))
    pl.when(has_below)(lambda: greet({"cuts": cut - 1}))
    pl.when(has_above)(lambda: greet({"cuts": cut + 1}))

    for l in range(2):
        zf[1, l] = jnp.zeros((k, width), F32)

    @pl.when(jnp.logical_not(has_next))
    def _():
        rz[...] = jnp.zeros_like(rz)

    @pl.when(jnp.logical_not(has_prev))
    def _():
        rp[...] = jnp.zeros_like(rp)

    @pl.when(jnp.logical_not(has_below))
    def _():
        high_in[...] = jnp.zeros_like(high_in)
        tail_in[...] = jnp.zeros_like(tail_in)
        cross_in[...] = jnp.zeros_like(cross_in)

    @pl.when(jnp.logical_not(has_above))
    def _():
        ylow_in[...] = jnp.zeros_like(ylow_in)

    bounds_load.wait()
    low = bounds[0, 0].astype(F32) / 64.0
    high = bounds[0, 1].astype(F32) / 64.0
    centre = jnp.full((8, 128), (low + high) / 2.0, F32)[:1, :1]
    inverse = 1.0 / jnp.full((8, 128), (high - low) / 2.0, F32)[:1, :1]
    def take(l):
        mine = x_own[:, l, :]
        zf[0, l] = mine
        zb[0, l] = mine.astype(BF16)

    x_load.wait()
    take(0)
    greeted = 2 + jnp.where(has_below, 1, 0) + jnp.where(has_above, 1, 0)
    pl.semaphore_wait(barrier, greeted)

    rounds = ready.shape[0]

    def tell(r):
        for step in (1 << r, -(1 << r)):
            pl.semaphore_signal(
                ready.at[r], inc=1, device_id=ring(step), device_id_type=MESH
            )

    def hear(r):
        pl.semaphore_wait(ready.at[r], 2)

    columns = [pl.ds(h * part, part) for h in range(PARTS)]

    def remote(src, dst, send, recv, device):
        return pltpu.make_async_remote_copy(
            src, dst, send, recv, device_id=device, device_id_type=MESH
        )

    def z_copy(t, h):
        return remote(
            zb.at[t, 0, :, columns[h]], rz.at[t, :, columns[h]], zs.at[t, h], zr.at[t, h],
            {"layer": me - 1},
        )

    def p_copy(t, h):
        return remote(
            pb.at[t, h], rp.at[t, h], ps.at[t, h], pr.at[t, h], {"layer": me + 1}
        )

    lengths = [pl.ds(0, rows) for rows in (3 * k // 8, 3 * k // 8, EDGE)]

    def group_copy(i, q):
        return remote(
            own.at[i, 0, lengths[i]], first.at[i, q, lengths[i]],
            a1s.at[i, q], a1r.at[i, q], {"layer": group_peer[q]},
        )

    def plane_copy(i, q):
        return remote(
            own.at[i, 1, lengths[i]], second.at[i, q, lengths[i]],
            a2s.at[i, q], a2r.at[i, q], {"layer": plane_peer[q]},
        )

    def reduce_start(i, value):
        own[i, 0, lengths[i]] = value
        for q in range(GROUP - 1):
            group_copy(i, q).start()

    def reduce_middle(i):
        for q in range(GROUP - 1):
            group_copy(i, q).wait_recv()
        total = own[i, 0, lengths[i]]
        for q in range(GROUP - 1):
            total = total + first[i, q, lengths[i]]
        own[i, 1, lengths[i]] = total
        for q in range(n_z - 1):
            plane_copy(i, q).start()

    def reduce_end(i):
        for q in range(n_z - 1):
            plane_copy(i, q).wait_recv()
        total = own[i, 1, lengths[i]]
        for q in range(n_z - 1):
            total = total + second[i, q, lengths[i]]
        return total

    def gram_start(i, grams):
        gram = grams[0] + grams[1]
        reduce_start(i, pack_symmetric(gram[:k, :k] + gram[:k, k:] + gram[k:, :k]))

    def gram_end(i):
        return unpack_symmetric(reduce_end(i), k) * scale

    def first_gram():
        pairs = [jnp.concatenate(split(zf[0, l]), axis=0) for l in range(2)]
        gram_start(0, [mm(pair, pair, NT) for pair in pairs])

    core = member % 2

    def close_low(l):
        stack[l] = stacked_rows(zf[0, l])
        ylow_out[l] = mm(factors[:EDGE], stack[l]).astype(BF16)

    def close_rest(l):
        stack[l] = stacked_rows(mm(factors[...], stack[l]))
        pair = stack[l, : 2 * k]
        return mm(pair, pair, NT)

    runs = STEPS * DEG

    def send_product(t):
        for h, s in enumerate(columns):
            pb[t, h] = mm(zb[t, 1], cv[1, :, s]).astype(BF16)
            pl.when(has_next)(lambda: p_copy(t, h).start())

    def apply_step(t, carry):
        cur, nxt = t % 2, (t + 1) % 2
        opening = t % DEG == 0
        factor, back = jnp.where(opening, 1.0, 2.0), jnp.where(opening, 0.0, 1.0)
        more = t + 1 < runs

        for r in range(rounds):

            @pl.when(t == r + 1)
            def _():
                hear(r)
                if r + 1 < rounds:
                    tell(r + 1)

        pl.when(t == DEG)(first_gram)
        pl.when(t == DEG + 1)(lambda: reduce_middle(0))

        acc[0] = mm(zb[t, 0], dv[0]) + mm(zb[t, 1], ct[0])
        acc[1] = mm(zb[t, 1], dv[1]) + mm(zb[t, 0], cv[0])

        @pl.when(t == runs - 2)
        def _():
            gram_first[...] = gram_end(0)

        @pl.when(t == runs - 1)
        def _():
            factors[...] = stacked_factor(cholesky_inverse(gram_first[...]))

        def update(l, s, total):
            now = zf[cur, l, :, s]
            value = (factor * inverse) * (total - centre * now) - back * zf[nxt, l, :, s]
            zf[nxt, l, :, s] = value
            zb[t + 1, l, :, s] = value.astype(BF16)

        def finish_first():
            for h, s in enumerate(columns):
                pl.when(has_prev)(lambda: p_copy(t, h).wait_recv())
                update(0, s, acc[0, :, s] + rp[t, h].astype(F32))
                pl.when(jnp.logical_and(has_prev, more))(lambda: z_copy(t + 1, h).start())

        def close_early():
            close_low(1 - core)
            gram_part[...] = close_rest(1 - core)

        early = jnp.logical_and(t == runs - 1, core == 1)

        @pl.when(early)
        def _():
            finish_first()
            close_early()

        for h, s in enumerate(columns):
            pl.when(has_next)(lambda: z_copy(t, h).wait_recv())
            total = acc[1] + mm(rz[t, :, s], ct[1, s, :])
            if h + 1 < PARTS:
                acc[1] = total
            else:
                update(1, pl.ds(0, width), total)

        pl.when(more)(lambda: send_product(t + 1))
        pl.when(jnp.logical_and(t == runs - 1, core == 0))(close_early)
        pl.when(jnp.logical_not(early))(finish_first)
        return carry

    for h in range(PARTS):
        pl.when(has_prev)(lambda: z_copy(0, h).start())
    take(1)
    tell(0)
    loads[0].wait()
    send_product(0)
    for copy in loads[1:]:
        copy.wait()
    for l in (1, 0):
        ct[l] = jnp.transpose(cv[l])
    lax.fori_loop(0, runs, apply_step, 0)

    below, above = {"cuts": cut - 1}, {"cuts": cut + 1}
    ylow_copy = remote(ylow_out, ylow_in, es.at[0], er.at[0], below)
    tail_copy = remote(tail_out, tail_in, es.at[1], er.at[1], above)
    cross_copies = [
        remote(
            own.at[2, 1, lengths[2]], cross_in.at[q], xs.at[q], xr.at[q],
            {"cuts": cut + 1, "layer": ((plane + q) % n_z) * GROUP + member},
        )
        for q in far_first + [0]
    ]
    high_copies = [
        remote(high_out.at[l], high_in.at[l], es.at[2 + l], er.at[2 + l], above) for l in range(2)
    ]
    close_low(core)
    pl.when(has_below)(ylow_copy.start)
    gram_start(1, [close_rest(core), gram_part[...]])
    reduce_middle(1)

    pl.when(has_above)(ylow_copy.wait_recv)
    cross = jnp.zeros((EDGE, k), F32)
    corner = jnp.zeros((EDGE, EDGE), F32)
    for l in range(2):
        cross = cross + mm(ylow_in[l], stack[l, :k], NT) + mm(ylow_in[l], stack[l, k : 2 * k], NT)
        corner = corner + mm(ylow_in[l], ylow_in[l], NT)
    blank = jnp.zeros((EDGE, 128 - k - EDGE), F32)
    reduce_start(2, jnp.concatenate([cross, corner, blank], axis=1))
    reduce_middle(2)

    @pl.when(has_above)
    def _():
        for copy in cross_copies:
            copy.start()

    factor = cholesky_inverse(gram_end(1))
    factor_edge = factor[k - EDGE :]
    edge_rows = stacked_factor(factor_edge)
    tail_out[...] = jnp.concatenate([factor_edge, jnp.zeros((EDGE, 128 - k), F32)], axis=1)
    pl.when(has_above)(tail_copy.start)
    for l in range(2):
        high_out[l] = mm(edge_rows, stack[l]).astype(BF16)
        pl.when(has_above)(high_copies[l].start)
    all_rows = stacked_factor(factor)
    for l in range(2):
        zf[1, l] = mm(all_rows, stack[l])
        out[EDGE : k - EDGE, l, :] = zf[1, l, EDGE : k - EDGE]

    packed = reduce_end(2) * scale
    projected = exact(packed[:, :k], factor_edge, NT)
    corner = packed[:, k : k + EDGE]
    rows_at = lax.broadcasted_iota(jnp.int32, (EDGE, EDGE), 0)
    lanes_at = lax.broadcasted_iota(jnp.int32, (EDGE, EDGE), 1)
    corner = jnp.where(has_above, corner, (rows_at == lanes_at).astype(F32))
    above_factor = cholesky_inverse(corner)
    corr = exact(above_factor, projected, NN)
    w_high, w_low = split(exact(corr, above_factor, TN))
    for l in range(2):
        change = mm(w_high, ylow_in[l]) + mm(w_low, ylow_in[l])
        out[k - EDGE :, l, :] = zf[1, l, k - EDGE :] - change

    @pl.when(has_below)
    def _():
        tail_copy.wait_recv()
        for copy in cross_copies:
            copy.wait_recv()

    cross = cross_in[0]
    for q in range(1, n_z):
        cross = cross + cross_in[q]
    projected = exact(cross[:, :k] * scale, tail_in[:, :k], NT)
    c_high, c_low = split(exact(factor[:EDGE, :EDGE], projected, NN))
    for l in range(2):
        pl.when(has_below)(high_copies[l].wait_recv)
        change = mm(c_high, high_in[l]) + mm(c_low, high_in[l])
        out[:EDGE, l, :] = zf[1, l, :EDGE] - change

    pl.when(has_below)(ylow_copy.wait_send)
    for copy in [tail_copy] + high_copies + cross_copies:
        pl.when(has_above)(copy.wait_send)
    for i in range(3):
        for q in range(GROUP - 1):
            group_copy(i, q).wait_send()
        for q in range(n_z - 1):
            plane_copy(i, q).wait_send()

    def drain(t, carry):
        for h in range(PARTS):
            pl.when(has_prev)(lambda: z_copy(t, h).wait_send())
            pl.when(has_next)(lambda: p_copy(t, h).wait_send())
        return carry

    lax.fori_loop(0, runs, drain, 0)


def per_device(sizes, vectors, diag_blocks, couplings, bounds):
    x = vectors[0]
    k, _, width = x.shape
    n_z = sizes[1] // GROUP
    runs = STEPS * DEG
    rounds = (sizes[1] // 2).bit_length() - 1
    vmem = pl.BlockSpec(memory_space=pltpu.VMEM)
    hbm = pl.BlockSpec(memory_space=pltpu.HBM)
    dma = pltpu.SemaphoreType.DMA
    result = pl.pallas_call(
        functools.partial(kernel, sizes),
        out_shape=jax.ShapeDtypeStruct(x.shape, F32),
        in_specs=[hbm] * 4,
        out_specs=vmem,
        scratch_shapes=[
            pltpu.SMEM((1, 2), jnp.int32),
            pltpu.VMEM((k, 2, width), F32),
            pltpu.VMEM((2, width, width), BF16),
            pltpu.VMEM((2, width, width), BF16),
            pltpu.VMEM((2, width, width), BF16),
            pltpu.VMEM((2, 2, k, width), F32),
            pltpu.VMEM((runs + 1, 2, k, width), BF16),
            pltpu.VMEM((runs, PARTS, k, width // PARTS), BF16),
            pltpu.VMEM((runs, k, width), BF16),
            pltpu.VMEM((runs, PARTS, k, width // PARTS), BF16),
            pltpu.VMEM((2, k, width), F32),
            pltpu.VMEM((3, 2, 3 * k // 8, 128), F32),
            pltpu.VMEM((3, GROUP - 1, 3 * k // 8, 128), F32),
            pltpu.VMEM((3, n_z - 1, 3 * k // 8, 128), F32),
            pltpu.VMEM((k, 3 * k), BF16),
            pltpu.VMEM((2, 3 * k, width), BF16),
            pltpu.VMEM((2 * k, 2 * k), F32),
            pltpu.VMEM((k, k), F32),
            pltpu.VMEM((2, EDGE, width), BF16),
            pltpu.VMEM((2, EDGE, width), BF16),
            pltpu.VMEM((2, EDGE, width), BF16),
            pltpu.VMEM((2, EDGE, width), BF16),
            pltpu.VMEM((EDGE, 128), F32),
            pltpu.VMEM((EDGE, 128), F32),
            pltpu.VMEM((n_z, EDGE, 128), F32),
            dma((6,)),
            dma((runs, PARTS)),
            dma((runs, PARTS)),
            dma((runs, PARTS)),
            dma((runs, PARTS)),
            dma((3, GROUP - 1)),
            dma((3, GROUP - 1)),
            dma((3, n_z - 1)),
            dma((3, n_z - 1)),
            dma((4,)),
            dma((4,)),
            dma((n_z,)),
            dma((n_z,)),
            pltpu.SemaphoreType.REGULAR((rounds,)),
        ],
        compiler_params=pltpu.CompilerParams(
            collective_id=0, has_side_effects=True, vmem_limit_bytes=48 << 20
        ),
    )(*(
        pltpu.with_memory_space_constraint(operand, pltpu.HBM)
        for operand in (bounds, x, diag_blocks, couplings)
    ))
    return result[None]


def solution(mesh):
    sizes = (mesh.shape["cuts"], mesh.shape["layer"])
    in_specs = (
        P("cuts", None, "layer", None),
        P("layer", None, None),
        P("layer", None, None),
        P("cuts", None),
    )
    return jax.shard_map(
        functools.partial(per_device, sizes),
        mesh=mesh,
        in_specs=in_specs,
        out_specs=P("cuts", None, "layer", None),
        check_vma=False,
    )
```

```python
import functools

import jax
import jax.numpy as jnp
from jax import lax
from jax.experimental import pallas as pl
from jax.experimental.pallas import tpu as pltpu
from jax.sharding import PartitionSpec as P

EDGE = 16
DEG = 4
STEPS = 2
PARTS = 4
GROUP = 4
F32 = jnp.float32
BF16 = jnp.bfloat16
NN = (((1,), (0,)), ((), ()))
NT = (((1,), (1,)), ((), ()))
TN = (((0,), (0,)), ((), ()))
MESH = pl.DeviceIdType.MESH


def mm(a, b, dims=NN):
    return lax.dot_general(a, b, dims, preferred_element_type=F32)


def split(value):
    high = value.astype(BF16)
    return high, (value - high.astype(F32)).astype(BF16)


def cholesky_inverse(gram, group=8):
    n = gram.shape[0]
    rows_at = lax.broadcasted_iota(jnp.int32, (n, n), 0)
    lanes_at = lax.broadcasted_iota(jnp.int32, (n, n), 1)
    eye = (rows_at == lanes_at).astype(F32)
    whole = jnp.concatenate([gram, eye], axis=1)
    shape = (8, 2 * n)
    blocks = [whole[8 * b : 8 * b + 8] for b in range(n // 8)]
    inner = lax.broadcasted_iota(jnp.int32, shape, 0)
    for j in range(0, n, group):
        home, at = j // 8, j % 8
        active = range(home, n // 8)
        rows = [jnp.broadcast_to(blocks[home][at + i : at + i + 1], shape) for i in range(group)]
        cross = {
            (i, m): jnp.broadcast_to(rows[i][:, j + m : j + m + 1], shape)
            for i in range(group)
            for m in range(i, group)
        }
        columns = {
            (b, i): jnp.broadcast_to(blocks[b][:, j + i : j + i + 1], shape)
            for b in active
            for i in range(group)
        }
        for i in range(group):
            inverse = 1.0 / cross[i, i]
            scaled = rows[i] * inverse
            later = range(i + 1, group)
            ratio = {m: cross[i, m] * inverse for m in later}
            for m in later:
                rows[m] = rows[m] - cross[i, m] * scaled
                for q in range(m, group):
                    cross[m, q] = cross[m, q] - cross[i, m] * ratio[q]
            for b in active:
                column = columns[b, i]
                for m in later:
                    columns[b, m] = columns[b, m] - column * ratio[m]
                if b == home:
                    column = jnp.where(inner > at + i, column, 0.0)
                blocks[b] = blocks[b] - column * scaled
    whole = jnp.concatenate(blocks, axis=0)
    diagonal = jnp.sum(whole[:, :n] * eye, axis=1, keepdims=True)
    return whole[:, n:] * lax.rsqrt(diagonal)


def stacked_factor(factor):
    high, low = split(factor)
    return jnp.concatenate([high, high, low], axis=1)


def stacked_rows(rows):
    high, low = split(rows)
    return jnp.concatenate([high, low, high], axis=0)


def pack_symmetric(gram):
    q = gram.shape[0] // 2
    quarters = (gram[:q, :q], gram[q:, :q], gram[q:, q:])
    cut = 3 * q // 4
    tail = jnp.concatenate([block[cut:] for block in quarters], axis=0)
    return jnp.concatenate([block[:cut] for block in quarters] + [tail], axis=1)


def unpack_symmetric(packed, k):
    q = k // 2
    rest = q // 4
    top, side, bottom = (
        jnp.concatenate(
            [packed[:, q * i : q * (i + 1)], packed[rest * i : rest * (i + 1), 3 * q :]], axis=0
        )
        for i in range(3)
    )
    upper = jnp.concatenate([top, jnp.transpose(side)], axis=1)
    return jnp.concatenate([upper, jnp.concatenate([side, bottom], axis=1)], axis=0)


def exact(a, b, dims):
    return lax.dot_general(
        a, b, dims, precision=lax.Precision.HIGHEST, preferred_element_type=F32
    )


def kernel(
    sizes, bounds_hbm, x_in, d_hbm, c_hbm, out,
    bounds, x_own, dv, cv, ct, zf, zb, pb, rz, rp, acc, own, first, second, factors, stack,
    ylow_out, ylow_in, high_out, high_in, tail_out, tail_in, cross_in,
    load_sem, zs, zr, ps, pr, a1s, a1r, a2s, a2r, es, er, xs, xr, ready,
):
    n_cuts, n_layer = sizes
    n_z = n_layer // GROUP
    me = lax.axis_index("layer")
    cut = lax.axis_index("cuts")
    plane, member = me // GROUP, me % GROUP
    k, _, width = x_in.shape
    part = width // PARTS
    scale = 1.0 / (n_layer * 2 * width)
    has_prev, has_next = me > 0, me < n_layer - 1
    has_below, has_above = cut > 0, cut < n_cuts - 1
    group_peer = [plane * GROUP + (member + q) % GROUP for q in range(1, GROUP)]
    far_first = sorted(range(1, n_z), key=lambda q: -min(q, n_z - q))
    plane_peer = [((plane + q) % n_z) * GROUP + member for q in far_first]

    x_load = pltpu.make_async_copy(x_in, x_own, load_sem.at[5])
    x_load.start()
    bounds_load = pltpu.make_async_copy(bounds_hbm, bounds, load_sem.at[4])
    bounds_load.start()
    loads = []
    for i, (src, dst) in enumerate(((c_hbm, cv), (d_hbm, dv))):
        for l in (1, 0):
            loads.append(pltpu.make_async_copy(src.at[l], dst.at[l], load_sem.at[2 * i + l]))
    loads[0].start()

    barrier = pltpu.get_barrier_semaphore()

    def ring(step):
        return {"layer": (me + step + n_layer) % n_layer}

    def greet(device):
        pl.semaphore_signal(barrier, inc=1, device_id=device, device_id_type=MESH)

    greet(ring(1))
    greet(ring(-1))
    pl.when(has_below)(lambda: greet({"cuts": cut - 1}))
    pl.when(has_above)(lambda: greet({"cuts": cut + 1}))

    for l in range(2):
        zf[1, l] = jnp.zeros((k, width), F32)

    @pl.when(jnp.logical_not(has_next))
    def _():
        rz[...] = jnp.zeros_like(rz)

    @pl.when(jnp.logical_not(has_prev))
    def _():
        rp[...] = jnp.zeros_like(rp)

    @pl.when(jnp.logical_not(has_below))
    def _():
        high_in[...] = jnp.zeros_like(high_in)
        tail_in[...] = jnp.zeros_like(tail_in)
        cross_in[...] = jnp.zeros_like(cross_in)

    @pl.when(jnp.logical_not(has_above))
    def _():
        ylow_in[...] = jnp.zeros_like(ylow_in)

    bounds_load.wait()
    low = bounds[0, 0].astype(F32) / 64.0
    high = bounds[0, 1].astype(F32) / 64.0
    centre = jnp.full((8, 128), (low + high) / 2.0, F32)[:1, :1]
    inverse = 1.0 / jnp.full((8, 128), (high - low) / 2.0, F32)[:1, :1]
    def take(l):
        mine = x_own[:, l, :]
        zf[0, l] = mine
        zb[0, l] = mine.astype(BF16)

    x_load.wait()
    take(0)
    greeted = 2 + jnp.where(has_below, 1, 0) + jnp.where(has_above, 1, 0)
    pl.semaphore_wait(barrier, greeted)

    rounds = ready.shape[0]

    def tell(r):
        for step in (1 << r, -(1 << r)):
            pl.semaphore_signal(
                ready.at[r], inc=1, device_id=ring(step), device_id_type=MESH
            )

    def hear(r):
        pl.semaphore_wait(ready.at[r], 2)

    columns = [pl.ds(h * part, part) for h in range(PARTS)]

    def remote(src, dst, send, recv, device):
        return pltpu.make_async_remote_copy(
            src, dst, send, recv, device_id=device, device_id_type=MESH
        )

    def z_copy(t, h):
        return remote(
            zb.at[t, 0, :, columns[h]], rz.at[t, :, columns[h]], zs.at[t, h], zr.at[t, h],
            {"layer": me - 1},
        )

    def p_copy(t, h):
        return remote(
            pb.at[t, h], rp.at[t, h], ps.at[t, h], pr.at[t, h], {"layer": me + 1}
        )

    lengths = [pl.ds(0, rows) for rows in (3 * k // 8, 3 * k // 8, EDGE)]

    def group_copy(i, q):
        return remote(
            own.at[i, 0, lengths[i]], first.at[i, q, lengths[i]],
            a1s.at[i, q], a1r.at[i, q], {"layer": group_peer[q]},
        )

    def plane_copy(i, q):
        return remote(
            own.at[i, 1, lengths[i]], second.at[i, q, lengths[i]],
            a2s.at[i, q], a2r.at[i, q], {"layer": plane_peer[q]},
        )

    def reduce_start(i, value):
        own[i, 0, lengths[i]] = value
        for q in range(GROUP - 1):
            group_copy(i, q).start()

    def reduce_middle(i):
        for q in range(GROUP - 1):
            group_copy(i, q).wait_recv()
        total = own[i, 0, lengths[i]]
        for q in range(GROUP - 1):
            total = total + first[i, q, lengths[i]]
        own[i, 1, lengths[i]] = total
        for q in range(n_z - 1):
            plane_copy(i, q).start()

    def reduce_end(i):
        for q in range(n_z - 1):
            plane_copy(i, q).wait_recv()
        total = own[i, 1, lengths[i]]
        for q in range(n_z - 1):
            total = total + second[i, q, lengths[i]]
        return total

    def gram_start(i, pairs):
        gram = jnp.zeros((2 * k, 2 * k), F32)
        for pair in pairs:
            gram = gram + mm(pair, pair, NT)
        reduce_start(i, pack_symmetric(gram[:k, :k] + gram[:k, k:] + gram[k:, :k]))

    def gram_end(i):
        return unpack_symmetric(reduce_end(i), k) * scale

    def first_gram():
        gram_start(0, [jnp.concatenate(split(zf[0, l]), axis=0) for l in range(2)])

    runs = STEPS * DEG

    def send_product(t):
        for h, s in enumerate(columns):
            pb[t, h] = mm(zb[t, 1], cv[1, :, s]).astype(BF16)
            pl.when(has_next)(lambda: p_copy(t, h).start())

    def apply_step(t, carry):
        cur, nxt = t % 2, (t + 1) % 2
        opening = t % DEG == 0
        factor, back = jnp.where(opening, 1.0, 2.0), jnp.where(opening, 0.0, 1.0)
        more = t + 1 < runs

        for r in range(rounds):

            @pl.when(t == r + 1)
            def _():
                hear(r)
                if r + 1 < rounds:
                    tell(r + 1)

        pl.when(t == DEG)(first_gram)

        acc[0] = mm(zb[t, 0], dv[0]) + mm(zb[t, 1], ct[0])
        acc[1] = mm(zb[t, 1], dv[1]) + mm(zb[t, 0], cv[0])

        pl.when(t == DEG + 1)(lambda: reduce_middle(0))

        @pl.when(t == runs - 1)
        def _():
            factors[...] = stacked_factor(cholesky_inverse(gram_end(0)))

        def update(l, s, total):
            now = zf[cur, l, :, s]
            value = (factor * inverse) * (total - centre * now) - back * zf[nxt, l, :, s]
            zf[nxt, l, :, s] = value
            zb[t + 1, l, :, s] = value.astype(BF16)

        for h, s in enumerate(columns):
            pl.when(has_next)(lambda: z_copy(t, h).wait_recv())
            total = acc[1] + mm(rz[t, :, s], ct[1, s, :])
            if h + 1 < PARTS:
                acc[1] = total
            else:
                update(1, pl.ds(0, width), total)

        pl.when(more)(lambda: send_product(t + 1))

        for h, s in enumerate(columns):
            pl.when(has_prev)(lambda: p_copy(t, h).wait_recv())
            update(0, s, acc[0, :, s] + rp[t, h].astype(F32))
            pl.when(jnp.logical_and(has_prev, more))(lambda: z_copy(t + 1, h).start())
        return carry

    for h in range(PARTS):
        pl.when(has_prev)(lambda: z_copy(0, h).start())
    take(1)
    tell(0)
    loads[0].wait()
    for copy in loads[1:]:
        copy.start()
    send_product(0)
    for copy in loads[1:]:
        copy.wait()
    for l in (1, 0):
        ct[l] = jnp.transpose(cv[l])
    lax.fori_loop(0, runs, apply_step, 0)

    below, above = {"cuts": cut - 1}, {"cuts": cut + 1}
    ylow_copy = remote(ylow_out, ylow_in, es.at[0], er.at[0], below)
    tail_copy = remote(tail_out, tail_in, es.at[1], er.at[1], above)
    cross_copies = [
        remote(
            own.at[2, 1, lengths[2]], cross_in.at[q], xs.at[q], xr.at[q],
            {"cuts": cut + 1, "layer": ((plane + q) % n_z) * GROUP + member},
        )
        for q in far_first + [0]
    ]
    high_copies = [
        remote(high_out.at[l], high_in.at[l], es.at[2 + l], er.at[2 + l], above) for l in range(2)
    ]
    for l in range(2):
        stack[l] = stacked_rows(zf[0, l])
        ylow_out[l] = mm(factors[:EDGE], stack[l]).astype(BF16)
    pl.when(has_below)(ylow_copy.start)
    for l in range(2):
        stack[l] = stacked_rows(mm(factors[...], stack[l]))
    gram_start(1, [stack[l, : 2 * k] for l in range(2)])
    reduce_middle(1)

    pl.when(has_above)(ylow_copy.wait_recv)
    cross = jnp.zeros((EDGE, k), F32)
    corner = jnp.zeros((EDGE, EDGE), F32)
    for l in range(2):
        cross = cross + mm(ylow_in[l], stack[l, :k], NT) + mm(ylow_in[l], stack[l, k : 2 * k], NT)
        corner = corner + mm(ylow_in[l], ylow_in[l], NT)
    blank = jnp.zeros((EDGE, 128 - k - EDGE), F32)
    reduce_start(2, jnp.concatenate([cross, corner, blank], axis=1))
    reduce_middle(2)

    @pl.when(has_above)
    def _():
        for copy in cross_copies:
            copy.start()

    factor = cholesky_inverse(gram_end(1))
    factor_edge = factor[k - EDGE :]
    edge_rows = stacked_factor(factor_edge)
    tail_out[...] = jnp.concatenate([factor_edge, jnp.zeros((EDGE, 128 - k), F32)], axis=1)
    pl.when(has_above)(tail_copy.start)
    for l in range(2):
        high_out[l] = mm(edge_rows, stack[l]).astype(BF16)
        pl.when(has_above)(high_copies[l].start)
    all_rows = stacked_factor(factor)
    for l in range(2):
        zf[1, l] = mm(all_rows, stack[l])
        out[EDGE : k - EDGE, l, :] = zf[1, l, EDGE : k - EDGE]

    packed = reduce_end(2) * scale
    projected = exact(packed[:, :k], factor_edge, NT)
    corner = packed[:, k : k + EDGE]
    rows_at = lax.broadcasted_iota(jnp.int32, (EDGE, EDGE), 0)
    lanes_at = lax.broadcasted_iota(jnp.int32, (EDGE, EDGE), 1)
    corner = jnp.where(has_above, corner, (rows_at == lanes_at).astype(F32))
    above_factor = cholesky_inverse(corner)
    corr = exact(above_factor, projected, NN)
    w_high, w_low = split(exact(corr, above_factor, TN))
    for l in range(2):
        change = mm(w_high, ylow_in[l]) + mm(w_low, ylow_in[l])
        out[k - EDGE :, l, :] = zf[1, l, k - EDGE :] - change

    @pl.when(has_below)
    def _():
        tail_copy.wait_recv()
        for copy in cross_copies:
            copy.wait_recv()

    cross = cross_in[0]
    for q in range(1, n_z):
        cross = cross + cross_in[q]
    projected = exact(cross[:, :k] * scale, tail_in[:, :k], NT)
    c_high, c_low = split(exact(factor[:EDGE, :EDGE], projected, NN))
    for l in range(2):
        pl.when(has_below)(high_copies[l].wait_recv)
        change = mm(c_high, high_in[l]) + mm(c_low, high_in[l])
        out[:EDGE, l, :] = zf[1, l, :EDGE] - change

    pl.when(has_below)(ylow_copy.wait_send)
    for copy in [tail_copy] + high_copies + cross_copies:
        pl.when(has_above)(copy.wait_send)
    for i in range(3):
        for q in range(GROUP - 1):
            group_copy(i, q).wait_send()
        for q in range(n_z - 1):
            plane_copy(i, q).wait_send()

    def drain(t, carry):
        for h in range(PARTS):
            pl.when(has_prev)(lambda: z_copy(t, h).wait_send())
            pl.when(has_next)(lambda: p_copy(t, h).wait_send())
        return carry

    lax.fori_loop(0, runs, drain, 0)


def per_device(sizes, vectors, diag_blocks, couplings, bounds):
    x = vectors[0]
    k, _, width = x.shape
    n_z = sizes[1] // GROUP
    runs = STEPS * DEG
    rounds = (sizes[1] // 2).bit_length() - 1
    vmem = pl.BlockSpec(memory_space=pltpu.VMEM)
    hbm = pl.BlockSpec(memory_space=pltpu.HBM)
    dma = pltpu.SemaphoreType.DMA
    result = pl.pallas_call(
        functools.partial(kernel, sizes),
        out_shape=jax.ShapeDtypeStruct(x.shape, F32),
        in_specs=[hbm] * 4,
        out_specs=vmem,
        scratch_shapes=[
            pltpu.SMEM((1, 2), jnp.int32),
            pltpu.VMEM((k, 2, width), F32),
            pltpu.VMEM((2, width, width), BF16),
            pltpu.VMEM((2, width, width), BF16),
            pltpu.VMEM((2, width, width), BF16),
            pltpu.VMEM((2, 2, k, width), F32),
            pltpu.VMEM((runs + 1, 2, k, width), BF16),
            pltpu.VMEM((runs, PARTS, k, width // PARTS), BF16),
            pltpu.VMEM((runs, k, width), BF16),
            pltpu.VMEM((runs, PARTS, k, width // PARTS), BF16),
            pltpu.VMEM((2, k, width), F32),
            pltpu.VMEM((3, 2, 3 * k // 8, 128), F32),
            pltpu.VMEM((3, GROUP - 1, 3 * k // 8, 128), F32),
            pltpu.VMEM((3, n_z - 1, 3 * k // 8, 128), F32),
            pltpu.VMEM((k, 3 * k), BF16),
            pltpu.VMEM((2, 3 * k, width), BF16),
            pltpu.VMEM((2, EDGE, width), BF16),
            pltpu.VMEM((2, EDGE, width), BF16),
            pltpu.VMEM((2, EDGE, width), BF16),
            pltpu.VMEM((2, EDGE, width), BF16),
            pltpu.VMEM((EDGE, 128), F32),
            pltpu.VMEM((EDGE, 128), F32),
            pltpu.VMEM((n_z, EDGE, 128), F32),
            dma((6,)),
            dma((runs, PARTS)),
            dma((runs, PARTS)),
            dma((runs, PARTS)),
            dma((runs, PARTS)),
            dma((3, GROUP - 1)),
            dma((3, GROUP - 1)),
            dma((3, n_z - 1)),
            dma((3, n_z - 1)),
            dma((4,)),
            dma((4,)),
            dma((n_z,)),
            dma((n_z,)),
            pltpu.SemaphoreType.REGULAR((rounds,)),
        ],
        compiler_params=pltpu.CompilerParams(
            collective_id=0, has_side_effects=True, vmem_limit_bytes=48 << 20
        ),
    )(*(
        pltpu.with_memory_space_constraint(operand, pltpu.HBM)
        for operand in (bounds, x, diag_blocks, couplings)
    ))
    return result[None]


def solution(mesh):
    sizes = (mesh.shape["cuts"], mesh.shape["layer"])
    in_specs = (
        P("cuts", None, "layer", None),
        P("layer", None, None),
        P("layer", None, None),
        P("cuts", None),
    )
    return jax.shard_map(
        functools.partial(per_device, sizes),
        mesh=mesh,
        in_specs=in_specs,
        out_specs=P("cuts", None, "layer", None),
        check_vma=False,
    )
```
